256 devices in a mesh: dp: 8 (over z), seq: 32 (over y, x, core).
Axes of the slice: x: 4, y: 4, z: 8, core: 2. Of those that a mesh axis runs over, the one named last changes fastest.
Arguments:
- embeddings: bfloat16 [8, 16384, 512], P('dp', 'seq'), may hold values from -6 to 6
- user_ids: int32 [8, 16384], P('dp', 'seq'), may hold values from 0 to 63, never falling along the last dimension, each value on 1 to 512 neighbouring positions
- time_gaps: int32 [8, 16384], P('dp', 'seq'), may hold values from 0 to 16
- proj_weight: bfloat16 [512, 2048], replicated, may hold values from -0.25 to 0.25
- out_weight: bfloat16 [512, 512], replicated, may hold values from -0.25 to 0.25
- frequencies: float32 [64], replicated, may hold values from 0.001 to 0.1
- time_mix: float32 [4, 64], replicated, may hold values from -0.9 to 0.9
- cotangent: bfloat16 [8, 16384, 512], P('dp', 'seq'), may hold values from -6 to 6
Outputs:
- layer_out: bfloat16 [8, 16384, 512], P('dp', 'seq')
- grad_input: bfloat16 [8, 16384, 512], P('dp', 'seq')
- grad_proj: float32 [512, 2048], P('seq')
- grad_out_weight: float32 [512, 512], P('seq')
- grad_time_mix: float32 [4, 64], replicated
The draws below stay inside these ranges and needn't reach their ends.
Inputs may be any that keep to these rules, and one draw needn't show every extreme that they name: `user_ids`: within a stream the ids never fall, so each user's events are consecutive; a user holds at most 512 events, and some user holds exactly that many.
All inputs are finite; a program needn't handle non-finite values.
Results may differ from the reference program's by a relative error of at most 0.019.
Values may be sent and summed in bfloat16 or wider, within the bound.
A program may use at most 64 MiB of HBM per device.

```python
import math
import jax
import jax.numpy as jnp
import numpy as np
from jax import lax

D = 512
H = 4
NF = 64
E_DEV = 512
BLOCK = 512
REACH = 1
STREAMS = 8
EVENTS = 16384
N_SEQ = 32


def place_ends(values, rng, smallest, largest):
    index_at = [jax.random.randint(jax.random.fold_in(rng, axis), (), 0, length) for axis, length in enumerate(values.shape)]
    main_axis = values.shape.index(max(values.shape))
    next_to = index_at[:main_axis] + [(index_at[main_axis] + 1) % values.shape[main_axis]] + index_at[main_axis + 1:]
    return values.at[tuple(index_at)].set(smallest).at[tuple(next_to)].set(largest)


def block_levels(own_key, extent, pieces, least, top_value):
    def one(dim, blocks):
        draws = jax.random.uniform(jax.random.fold_in(jax.random.fold_in(own_key, 6), dim), (blocks,), jnp.float32, least / len(pieces), top_value / len(pieces))
        return jnp.repeat(jnp.exp(draws), extent[dim] // blocks).reshape((-1,) + (1,) * (len(extent) - dim - 1))

    loudness = one(*pieces[0])
    for cut in pieces[1:]:
        loudness = loudness * one(*cut)
    return loudness


def split_up(number_of, total, reach, lean):
    loads = [(1 << 20) // math.isqrt(rank ** lean) + 1 for rank in range(2, number_of + 1)]
    spare, holding = total - reach - (number_of - 1), [1] * (number_of - 1)
    while spare > 0:
        candidates = [i for i in range(number_of - 1) if holding[i] < reach]
        pool, remaining = sum([loads[i] for i in candidates]), spare
        for i in candidates:
            addition = min(reach - holding[i], max(1, remaining * loads[i] // pool), spare)
            holding[i] = holding[i] + addition
            spare = spare - addition
    return np.array([reach] + holding)


def ragged_sizes(rng, number_of, total, limit, skew):
    if number_of == 2:
        one = jax.random.randint(rng, (), max(1, total - limit), min(limit, total - 1) + 1)
        return jnp.stack([one, total - one])
    lengths = jnp.asarray(split_up(number_of, total, limit, skew), jnp.int32)
    couples = (number_of - 1) // 2
    source_of, taker = lengths[1:1 + 2 * couples:2], lengths[2:2 + 2 * couples:2]
    room = jnp.minimum(source_of - 1, limit - taker)
    shifted = jax.random.randint(jax.random.fold_in(rng, 1), (couples,), 0, 1 << 20) % (room + 1)
    lengths = lengths.at[1:1 + 2 * couples:2].set(source_of - shifted).at[2:2 + 2 * couples:2].set(taker + shifted)
    return lengths[jax.random.permutation(jax.random.fold_in(rng, 2), number_of)]


def gaussian(key, dims, width, limit, shards=(), held_as=jnp.bfloat16):
    values = jax.random.normal(key, dims, jnp.float32) * width
    if len(shards) > 0:
        values = block_levels(key, dims, shards, -0.22, 0.18) * values
    return jnp.clip(values, min=-limit, max=limit).astype(held_as)


def setup_inputs(seed: int = 0) -> dict:
    streams_of = jax.random.split(jax.random.key(seed), 9)
    return {
        "embeddings": gaussian(streams_of[0], (STREAMS, EVENTS, D), 1.0, 6.0, ((0, 8), (1, 32))),
        "user_ids": jax.vmap(lambda own: jnp.searchsorted(jnp.cumsum(ragged_sizes(own, 2 * N_SEQ, EVENTS, REACH * E_DEV, 1)), jnp.arange(EVENTS), side="right"))(jax.random.split(streams_of[1], STREAMS)).reshape((STREAMS, EVENTS)).astype(jnp.int32),
        "time_gaps": place_ends(jax.random.randint(streams_of[2], (STREAMS, EVENTS), 0, 17), jax.random.fold_in(streams_of[2], 1), 0, 16).astype(jnp.int32),
        "proj_weight": gaussian(streams_of[3], (D, 4 * D), D ** -0.5, 0.25),
        "out_weight": gaussian(streams_of[4], (D, D), D ** -0.5, 0.25),
        "frequencies": jnp.clip(jnp.exp(jax.random.uniform(streams_of[5], (NF,), jnp.float32, math.log(0.001), math.log(0.1))), 0.001, 0.1),
        "time_mix": gaussian(streams_of[6], (H, NF), 0.15, 0.9, (), jnp.float32),
        "cotangent": gaussian(streams_of[7], (STREAMS, EVENTS, D), 1.0, 6.0, ((0, 8), (1, 32))),
    }


EPSILON = 1e-05
HIGH = lax.Precision.HIGHEST

def silu_slope(value):
    sigma = jax.nn.sigmoid(value)
    return sigma * (1.0 + value * (1.0 - sigma))

def run_times(users, gaps):
    count = users.shape[0]
    running = jnp.cumsum(gaps).astype(jnp.int32)
    position = jnp.arange(count, dtype=jnp.int32)
    before = jnp.concatenate([users[:1] - 1, users[:-1]])
    opening = jnp.where(users != before, position, 0).astype(jnp.int32)
    first = lax.cummax(opening, axis=0)
    return (running - (running[first] - gaps[first])).astype(jnp.int32)

def time_features(times, frequencies, time_mix):
    angles = times.astype(jnp.float32)[:, None] * frequencies[None, :]
    cosines = jnp.cos(angles)
    sines = jnp.sin(angles)
    key_time = jnp.concatenate([cosines, sines], 1).astype(jnp.bfloat16)
    query_time = jnp.concatenate([cosines[:, None, :] * time_mix[None], sines[:, None, :] * time_mix[None]], 2).astype(jnp.bfloat16)
    return (cosines, sines, key_time, query_time)

def project(events, proj_weight):
    values_wide = events.astype(jnp.float32)
    scale_in = lax.rsqrt(lax.optimization_barrier(jnp.mean(values_wide * values_wide, -1, keepdims=True)) + EPSILON)
    unit_rows = values_wide * scale_in
    normed = unit_rows.astype(jnp.bfloat16)
    preact = jnp.dot(normed, proj_weight, preferred_element_type=jnp.float32)
    hidden = jax.nn.silu(preact).astype(jnp.bfloat16)
    return (scale_in, unit_rows, normed, preact, hidden)

def widen(array):
    return array.astype(jnp.float32)

def pair_scores(query, query_time, keys, key_time):
    inverse = query.shape[-1] ** (-0.5)
    return jnp.einsum('qhd,khd->hqk', widen(query), widen(keys), precision=HIGH) * inverse + jnp.einsum('qhf,kf->hqk', widen(query_time), widen(key_time), precision=HIGH)

def tile_rows(array, block):
    return lax.dynamic_slice_in_dim(array, (block * BLOCK).astype(jnp.int32), BLOCK, 0)

def stream_pass(events, users, gaps, upstream, proj_weight, out_weight, frequencies, time_mix):
    count = events.shape[0]
    model_width = events.shape[1]
    heads = time_mix.shape[0]
    head_size = model_width // heads
    freq_count = frequencies.shape[0]
    inverse = head_size ** (-0.5)
    times = run_times(users, gaps)
    cosines, sines, key_time, query_time = time_features(times, frequencies, time_mix)
    scale_in, unit_rows, normed, preact, hidden = project(events, proj_weight)
    gate_part = hidden[:, :model_width]
    value_heads = hidden[:, model_width:2 * model_width].reshape(count, heads, head_size)
    query_heads = hidden[:, 2 * model_width:3 * model_width].reshape(count, heads, head_size)
    key_heads = hidden[:, 3 * model_width:].reshape(count, heads, head_size)
    position = jnp.arange(count, dtype=jnp.int32)
    block_count = count // BLOCK
    reach_blocks = REACH * E_DEV // BLOCK

    def pair_terms(block, back):
        key_block = jnp.maximum(block - back, 0).astype(jnp.int32)
        mask = (tile_rows(users, key_block)[None, :] == tile_rows(users, block)[:, None]) & (tile_rows(position, key_block)[None, :] <= tile_rows(position, block)[:, None]) & (block - back >= 0)
        scores = pair_scores(tile_rows(query_heads, block), tile_rows(query_time, block), tile_rows(key_heads, key_block), tile_rows(key_time, key_block))
        weights = jnp.where(mask[None], jax.nn.silu(scores), 0.0).astype(jnp.bfloat16)
        return (key_block, mask, scores, weights)

    def forward_block(block):
        total = jnp.zeros((BLOCK, heads, head_size), jnp.float32)
        for back in range(reach_blocks + 1):
            key_block, mask, scores, weights = pair_terms(block, back)
            total = total + jnp.einsum('hqk,khd->qhd', widen(weights), widen(tile_rows(value_heads, key_block)), precision=HIGH)
        return total
    attended = lax.map(forward_block, jnp.arange(block_count, dtype=jnp.int32)).reshape(count, model_width)
    scale_mid = lax.rsqrt(lax.optimization_barrier(jnp.mean(attended * attended, -1, keepdims=True)) + EPSILON)
    normed_mid = attended * scale_mid
    gate_wide = gate_part.astype(jnp.float32)
    gated = (normed_mid * gate_wide).astype(jnp.bfloat16)
    layer_out = (events.astype(jnp.float32) + jnp.dot(gated, out_weight, preferred_element_type=jnp.float32)).astype(jnp.bfloat16)
    grad_gated = jnp.dot(upstream, out_weight.T, preferred_element_type=jnp.float32)
    grad_out_weight = jnp.dot(gated.T, upstream, preferred_element_type=jnp.float32)
    grad_gate = grad_gated * normed_mid
    grad_mid = grad_gated * gate_wide
    grad_attended = (scale_mid * (grad_mid - normed_mid * lax.optimization_barrier(jnp.mean(grad_mid * normed_mid, -1, keepdims=True)))).astype(jnp.bfloat16)
    grad_heads = grad_attended.reshape(count, heads, head_size)

    def backward_block(carry, block):
        grad_keys_all, grad_values_all = carry
        grad_query = jnp.zeros((BLOCK, heads, head_size), jnp.float32)
        grad_qtime = jnp.zeros((BLOCK, heads, 2 * freq_count), jnp.float32)
        grad_tile = widen(tile_rows(grad_heads, block))
        query_tile = widen(tile_rows(query_heads, block))
        for back in range(reach_blocks + 1):
            key_block, mask, scores, weights = pair_terms(block, back)
            key_tile = widen(tile_rows(key_heads, key_block))
            value_tile = widen(tile_rows(value_heads, key_block))
            grad_weights = jnp.einsum('qhd,khd->hqk', grad_tile, value_tile, precision=HIGH)
            grad_scores = widen(jnp.where(mask[None], grad_weights * silu_slope(scores), 0.0).astype(jnp.bfloat16))
            value_part = jnp.einsum('hqk,qhd->khd', widen(weights), grad_tile, precision=HIGH)
            key_part = jnp.einsum('hqk,qhd->khd', grad_scores, query_tile, precision=HIGH) * inverse
            grad_query = grad_query + jnp.einsum('hqk,khd->qhd', grad_scores, key_tile, precision=HIGH) * inverse
            grad_qtime = grad_qtime + jnp.einsum('hqk,kf->qhf', grad_scores, widen(tile_rows(key_time, key_block)), precision=HIGH)
            start = (key_block * BLOCK).astype(jnp.int32)
            grad_keys_all = lax.dynamic_update_slice_in_dim(grad_keys_all, tile_rows(grad_keys_all, key_block) + key_part, start, 0)
            grad_values_all = lax.dynamic_update_slice_in_dim(grad_values_all, tile_rows(grad_values_all, key_block) + value_part, start, 0)
        return ((grad_keys_all, grad_values_all), (grad_query, grad_qtime))
    empty = jnp.zeros((count, heads, head_size), jnp.float32)
    (grad_keys_all, grad_values_all), (grad_query, grad_qtime) = lax.scan(backward_block, (empty, empty), jnp.arange(block_count, dtype=jnp.int32))
    grad_query = grad_query.reshape(count, model_width)
    grad_qtime = grad_qtime.reshape(count, heads, 2 * freq_count)
    grad_act = jnp.concatenate([grad_gate, grad_values_all.reshape(count, model_width), grad_query, grad_keys_all.reshape(count, model_width)], 1)
    grad_pre = (grad_act * silu_slope(preact)).astype(jnp.bfloat16)
    grad_normed = jnp.dot(grad_pre, proj_weight.T, preferred_element_type=jnp.float32)
    grad_proj = jnp.dot(normed.T, grad_pre, preferred_element_type=jnp.float32)
    grad_input = (upstream.astype(jnp.float32) + scale_in * (grad_normed - unit_rows * lax.optimization_barrier(jnp.mean(grad_normed * unit_rows, -1, keepdims=True)))).astype(jnp.bfloat16)
    grad_mix = jnp.einsum('ehf,ef->hf', grad_qtime[:, :, :freq_count], cosines, precision=HIGH) + jnp.einsum('ehf,ef->hf', grad_qtime[:, :, freq_count:], sines, precision=HIGH)
    return (layer_out, grad_input, grad_proj, grad_out_weight, grad_mix)

def reference(embeddings, user_ids, time_gaps, proj_weight, out_weight, frequencies, time_mix, cotangent):
    model_width = embeddings.shape[2]
    heads = time_mix.shape[0]
    freq_count = frequencies.shape[0]

    def per_stream(totals, item):
        events, users, gaps, upstream = item
        results = stream_pass(events, users, gaps, upstream, proj_weight, out_weight, frequencies, time_mix)
        return ((totals[0] + results[2], totals[1] + results[3], totals[2] + results[4]), (results[0], results[1]))
    start = (jnp.zeros((model_width, 4 * model_width), jnp.float32), jnp.zeros((model_width, model_width), jnp.float32), jnp.zeros((heads, freq_count), jnp.float32))
    totals, outputs = lax.scan(per_stream, start, (embeddings, user_ids, time_gaps, cotangent))
    factor = float(STREAMS * EVENTS) ** (-0.5)
    return (outputs[0], outputs[1], totals[0] * factor, totals[1] * factor, totals[2] * factor)
```

```python
import functools

import jax
import jax.numpy as jnp
from jax import lax
from jax.experimental import pallas as pl
from jax.experimental.pallas import tpu as pltpu
from jax.sharding import PartitionSpec as P

EPS = 1e-05
F32 = jnp.float32
BF = jnp.bfloat16
N = 512
D = 512
H = 4
HD = 128
TQ = 256
WIN = 768
NCH = 5
MESH = pl.DeviceIdType.MESH


def nn(a, b):
    return lax.dot_general(a, b, (((1,), (0,)), ((), ())), preferred_element_type=F32)


def nt(a, b):
    return lax.dot_general(a, b, (((1,), (1,)), ((), ())), preferred_element_type=F32)


def tn(a, b):
    return lax.dot_general(a, b, (((0,), (0,)), ((), ())), preferred_element_type=F32)


def sigmoid(z):
    return 0.5 * jnp.tanh(0.5 * z) + 0.5


def kernel(
    n_dp,
    n_seq,
    x_ref,
    u_ref,
    g_ref,
    w_ref,
    wo_ref,
    f_ref,
    mix_ref,
    cot_ref,
    lo_ref,
    gi_ref,
    gp_out,
    go_out,
    gt_out,
    xprev,
    uprev,
    gprev,
    nrm,
    slope,
    slope_p,
    gate,
    kcat,
    qcat,
    v4,
    maskf,
    cs_own,
    wsav,
    slp,
    att4,
    gated_s,
    ga4,
    dk,
    dv,
    gpa,
    gpq,
    gpg,
    dq4,
    back_s,
    back_r,
    gf,
    s0_s,
    s0_r,
    s1_s,
    s1_r,
    z_r,
    t0_s,
    t0_r,
    t1_r,
    t2_r,
    halo_ss,
    halo_rs,
    back_ss,
    back_rs,
    st_ss,
    st_rs,
    tm_ss,
    tm_rs,
):
    n_yx = n_seq // 2
    rows = D // n_seq
    dp = lax.axis_index("dp")
    s = lax.axis_index("seq")
    core = lax.rem(s, 2)
    m = lax.div(s, 2)
    right = lax.rem(s + 1, n_seq)
    left = lax.rem(s + n_seq - 1, n_seq)
    partner = m * 2 + 1 - core

    def yx_dev(i):
        return (dp, i * 2 + core)

    def z_dev(i):
        return (i, s)

    barrier = pltpu.get_barrier_semaphore()
    for peer in (left, right, partner):
        pl.semaphore_signal(barrier, inc=1, device_id=(dp, peer), device_id_type=MESH)

    @pl.loop(1, n_yx)
    def _(k):
        peer = lax.rem(m + k, n_yx)
        pl.semaphore_signal(barrier, inc=1, device_id=yx_dev(peer), device_id_type=MESH)

    @pl.loop(1, n_dp)
    def _(k):
        peer = lax.rem(dp + k, n_dp)
        pl.semaphore_signal(barrier, inc=1, device_id=z_dev(peer), device_id_type=MESH)

    pl.semaphore_wait(barrier, 3 + (n_yx - 1) + (n_dp - 1))

    def remote(src, dst, ss, rs, dev):
        return pltpu.make_async_remote_copy(
            src_ref=src, dst_ref=dst, send_sem=ss, recv_sem=rs, device_id=dev, device_id_type=MESH
        )

    halo = [
        remote(u_ref, uprev, halo_ss.at[0], halo_rs.at[0], (dp, right)),
        remote(g_ref, gprev, halo_ss.at[1], halo_rs.at[1], (dp, right)),
        remote(x_ref, xprev, halo_ss.at[2], halo_rs.at[2], (dp, right)),
    ]
    for copy in halo:
        copy.start()

    def norm(x):
        wide = x.astype(F32)
        scale = lax.rsqrt(jnp.mean(wide * wide, -1, keepdims=True) + EPS)
        return wide, scale

    wide, scale = norm(x_ref[...])
    nrm[N:, :] = (wide * scale).astype(BF)

    def project(lo, group):
        p = nn(nrm[lo : lo + N, :], w_ref[:, group * D : (group + 1) * D])
        sg = sigmoid(p)
        hid = p * sg
        return hid.astype(BF), sg + hid * (1.0 - sg)

    def put_heads(dst, lo, val):
        for h in range(H):
            dst[h, lo : lo + N, :HD] = val[:, h * HD : (h + 1) * HD]

    hid, sl = project(N, 0)
    gate[...] = hid
    slope[:, 0:D] = sl
    hid, sl = project(N, 1)
    put_heads(v4, N, hid)
    slope[:, D : 2 * D] = sl
    hid, sl = project(N, 2)
    put_heads(qcat, 0, hid)
    slope[:, 2 * D : 3 * D] = sl
    hid, sl = project(N, 3)
    put_heads(kcat, N, hid)
    slope[:, 3 * D : 4 * D] = sl

    halo[0].wait_recv()
    halo[1].wait_recv()
    u_own = u_ref[...].astype(F32)
    u_prev = jnp.where(s == 0, -1.0, uprev[...].astype(F32))
    g_own = g_ref[...].astype(F32)
    g_prev = gprev[...].astype(F32)
    u_all = jnp.concatenate([u_prev, u_own], 1)
    g_all = jnp.broadcast_to(jnp.concatenate([g_prev, g_own], 1), (HD, 2 * N)).astype(BF)
    uc = jnp.transpose(jnp.broadcast_to(u_all, (HD, 2 * N)))[:, :1]
    freq = f_ref[...]
    lane = lax.broadcasted_iota(jnp.int32, (1, HD), 1)

    def features(times):
        ang = times * freq
        return jnp.where(lane < HD // 2, jnp.cos(ang), jnp.sin(ang))

    for a in range(N // TQ):
        q0, k0 = a * TQ, a * TQ
        kpos = lax.broadcasted_iota(jnp.int32, (TQ, WIN), 1) + k0
        qpos = lax.broadcasted_iota(jnp.int32, (TQ, WIN), 0) + (q0 + N)
        same = uc[N + q0 : N + q0 + TQ, :] == u_all[:, k0 : k0 + WIN]
        mk = jnp.where(same & (kpos <= qpos), 1.0, 0.0)
        maskf[q0 : q0 + TQ, :] = mk
        times = nt(mk.astype(BF), g_all[:, k0 : k0 + WIN])
        feat = features(times)
        cs_own[q0 : q0 + TQ, :] = feat
        fb = feat.astype(BF)
        for h in range(H):
            kcat[h, N + q0 : N + q0 + TQ, HD:] = fb
            qcat[h, q0 : q0 + TQ, HD:] = (feat * mix_ref[h : h + 1, :] * (HD**0.5)).astype(BF)
    pi = lax.broadcasted_iota(jnp.int32, (N, N), 0)
    pj = lax.broadcasted_iota(jnp.int32, (N, N), 1)
    mp = jnp.where((uc[:N, :] == u_all[:, :N]) & (pj <= pi), 1.0, 0.0).astype(BF)
    fb = features(nt(mp, g_all[:, :N])).astype(BF)
    for h in range(H):
        kcat[h, :N, HD:] = fb

    halo[2].wait_recv()
    wide, scale = norm(xprev[...])
    nrm[:N, :] = (wide * scale).astype(BF)
    hid, sl = project(0, 1)
    put_heads(v4, 0, hid)
    slope_p[:, :D] = sl
    hid, sl = project(0, 3)
    put_heads(kcat, 0, hid)
    slope_p[:, D:] = sl

    inv = HD**-0.5

    @pl.loop(0, H)
    def _(h):
        for a in range(N // TQ):
            q0, k0 = a * TQ, a * TQ
            z = nt(qcat[h, q0 : q0 + TQ, :], kcat[h, k0 : k0 + WIN, :]) * inv
            sg = sigmoid(z) * maskf[q0 : q0 + TQ, :]
            wt = z * sg
            slp[h, q0 : q0 + TQ, :] = sg + wt * (1.0 - sg)
            wb = wt.astype(BF)
            wsav[h, q0 : q0 + TQ, :] = wb
            att4[h, q0 : q0 + TQ, :] = nn(wb, v4[h, k0 : k0 + WIN, :])

    attended = jnp.concatenate([att4[h] for h in range(H)], 1)
    scale_mid = lax.rsqrt(jnp.mean(attended * attended, -1, keepdims=True) + EPS)
    normed_mid = attended * scale_mid
    gate_wide = gate[...].astype(F32)
    gated = (normed_mid * gate_wide).astype(BF)
    gated_s[...] = gated
    lo_ref[...] = (x_ref[...].astype(F32) + nn(gated, wo_ref[...])).astype(BF)
    grad_gated = nt(cot_ref[...], wo_ref[...])
    gpg[...] = (grad_gated * normed_mid * slope[:, :D]).astype(BF)
    grad_mid = grad_gated * gate_wide
    ga = (
        scale_mid * (grad_mid - normed_mid * jnp.mean(grad_mid * normed_mid, -1, keepdims=True))
    ).astype(BF)
    for h in range(H):
        ga4[h] = ga[:, h * HD : (h + 1) * HD]

    def stage0(c, g):
        g4 = g.reshape(n_yx, 2, rows, D)
        gf[c, 0] = g4[:, 0]
        gf[c, 1] = g4[:, 1]
        s0_s[c] = gf[c, 1 - core].astype(BF)
        remote(s0_s.at[c], s0_r.at[c], st_ss.at[0, c], st_rs.at[0, c], (dp, partner)).start()

    def stage1(c):
        remote(s0_s.at[c], s0_r.at[c], st_ss.at[0, c], st_rs.at[0, c], (dp, partner)).wait_recv()
        s1_s[c] = (gf[c, core] + s0_r[c].astype(F32)).astype(BF)
        s1_r[c, m] = s1_s[c, m]

        @pl.loop(1, n_yx)
        def _(k):
            peer = lax.rem(m + k, n_yx)
            remote(
                s1_s.at[c, peer], s1_r.at[c, m], st_ss.at[1, c], st_rs.at[1, c], yx_dev(peer)
            ).start()

    def wait_all(part, ss, rs, recv):
        copy = remote(part, part, ss, rs, (dp, partner))
        if recv:
            copy.wait_recv()
        else:
            copy.wait_send()

    yx_part = pl.ds(0, n_yx - 1)
    z_part = pl.ds(0, n_dp - 1)

    def stage2(c):
        wait_all(s1_r.at[c, yx_part], st_ss.at[1, c], st_rs.at[1, c], True)
        total = s1_r[c, 0].astype(F32)
        for i in range(1, n_yx):
            total = total + s1_r[c, i].astype(F32)
        z_r[c, dp] = total.astype(BF)

        @pl.loop(1, n_dp)
        def _(k):
            peer = lax.rem(dp + k, n_dp)
            remote(
                z_r.at[c, dp], z_r.at[c, dp], st_ss.at[2, c], st_rs.at[2, c], z_dev(peer)
            ).start()

    factor = float(n_dp * n_seq * N) ** -0.5

    def stage3(c):
        wait_all(z_r.at[c, z_part], st_ss.at[2, c], st_rs.at[2, c], True)
        total = z_r[c, 0].astype(F32)
        for i in range(1, n_dp):
            total = total + z_r[c, i].astype(F32)
        total = total * factor
        if c == 0:
            go_out[...] = total
        else:
            gp_out[:, (c - 1) * D : c * D] = total

    stage0(0, tn(gated_s[...], cot_ref[...]))
    stage0(1, tn(nrm[N:, :], gpg[...]))

    dk[...] = jnp.zeros_like(dk)
    dv[...] = jnp.zeros_like(dv)
    rowid = lax.broadcasted_iota(jnp.int32, (8, HD), 0)

    def head(h, tm):
        for a in range(N // TQ):
            q0, k0 = a * TQ, a * TQ
            gah = ga4[h, q0 : q0 + TQ, :]
            gw = nt(gah, v4[h, k0 : k0 + WIN, :])
            gs = (gw * slp[h, q0 : q0 + TQ, :]).astype(BF)
            dv[h, k0 : k0 + WIN, :] += tn(wsav[h, q0 : q0 + TQ, :], gah)
            dk[h, k0 : k0 + WIN, :] += tn(gs, qcat[h, q0 : q0 + TQ, :HD])
            dqc = nn(gs, kcat[h, k0 : k0 + WIN, :])
            dq4[h, q0 : q0 + TQ, :] = dqc[:, :HD]
            part = jnp.sum(dqc[:, HD:] * cs_own[q0 : q0 + TQ, :], 0, keepdims=True)
            tm = tm + jnp.where(rowid == h, part, 0.0)
        return tm

    tm = lax.fori_loop(0, H, head, jnp.zeros((8, HD), F32))
    t0_s[...] = tm
    tm0 = remote(t0_s, t0_r, tm_ss.at[0], tm_rs.at[0], (dp, partner))
    tm0.start()
    stage1(0)
    stage1(1)

    def join(ref, lo):
        return jnp.concatenate([ref[h, lo : lo + N, :] for h in range(H)], 1)

    gpa[0, :N, :] = (join(dv, 0) * slope_p[:, :D]).astype(BF)
    gpa[1, :N, :] = (join(dk, 0) * (slope_p[:, D:] * inv)).astype(BF)
    back_s[...] = (
        nt(gpa[0, :N, :], w_ref[:, D : 2 * D]) + nt(gpa[1, :N, :], w_ref[:, 3 * D :])
    ).astype(BF)
    back = remote(back_s, back_r, back_ss.at[0], back_rs.at[0], (dp, left))
    back.start()
    gpa[0, N:, :] = (join(dv, N) * slope[:, D : 2 * D]).astype(BF)
    gpa[1, N:, :] = (join(dk, N) * (slope[:, 3 * D :] * inv)).astype(BF)
    gpq[...] = (join(dq4, 0) * (slope[:, 2 * D : 3 * D] * inv)).astype(BF)
    stage0(2, tn(nrm[...], gpa[0]))
    stage0(3, tn(nrm[N:, :], gpq[...]))
    stage2(0)
    stage2(1)
    stage0(4, tn(nrm[...], gpa[1]))

    tm0.wait_recv()
    t1_r[m] = t0_s[...] + t0_r[...]

    @pl.loop(1, n_yx)
    def _(k):
        peer = lax.rem(m + k, n_yx)
        remote(t1_r.at[m], t1_r.at[m], tm_ss.at[1], tm_rs.at[1], yx_dev(peer)).start()

    stage1(2)
    stage1(3)
    stage1(4)
    gn = (
        nt(gpg[...], w_ref[:, :D])
        + nt(gpa[0, N:, :], w_ref[:, D : 2 * D])
        + nt(gpq[...], w_ref[:, 2 * D : 3 * D])
        + nt(gpa[1, N:, :], w_ref[:, 3 * D :])
    )
    wide, scale = norm(x_ref[...])
    unit = wide * scale
    stage2(2)
    stage2(3)
    stage2(4)
    wait_all(t1_r.at[yx_part], tm_ss.at[1], tm_rs.at[1], True)
    tsum = t1_r[0]
    for i in range(1, n_yx):
        tsum = tsum + t1_r[i]
    t2_r[dp] = tsum

    @pl.loop(1, n_dp)
    def _(k):
        peer = lax.rem(dp + k, n_dp)
        remote(t2_r.at[dp], t2_r.at[dp], tm_ss.at[2], tm_rs.at[2], z_dev(peer)).start()

    back.wait_recv()
    gn = gn + back_r[...].astype(F32)
    gi_ref[...] = (
        cot_ref[...].astype(F32) + scale * (gn - unit * jnp.mean(gn * unit, -1, keepdims=True))
    ).astype(BF)
    for c in range(NCH):
        stage3(c)
    wait_all(t2_r.at[z_part], tm_ss.at[2], tm_rs.at[2], True)
    tsum = t2_r[0]
    for i in range(1, n_dp):
        tsum = tsum + t2_r[i]
    tsum = (tsum + pltpu.roll(tsum, HD // 2, 1)) * factor
    gt_out[...] = tsum[:H, : HD // 2]

    for copy in halo:
        copy.wait_send()
    back.wait_send()
    tm0.wait_send()
    for c in range(NCH):
        remote(s0_s.at[c], s0_r.at[c], st_ss.at[0, c], st_rs.at[0, c], (dp, partner)).wait_send()
        wait_all(s1_r.at[c, yx_part], st_ss.at[1, c], st_rs.at[1, c], False)
        wait_all(z_r.at[c, z_part], st_ss.at[2, c], st_rs.at[2, c], False)
    wait_all(t1_r.at[yx_part], tm_ss.at[1], tm_rs.at[1], False)
    wait_all(t2_r.at[z_part], tm_ss.at[2], tm_rs.at[2], False)


def body(n_dp, n_seq, embeddings, user_ids, time_gaps, proj, out_w, freqs, mix, cot):
    n_yx = n_seq // 2
    rows = D // n_seq
    freq2 = jnp.concatenate([freqs, freqs])[None]
    mix2 = jnp.concatenate([mix, mix], 1)
    vm = pltpu.VMEM
    dma = pltpu.SemaphoreType.DMA
    scratch = [
        vm((N, D), BF),
        vm((1, N), jnp.int32),
        vm((1, N), jnp.int32),
        vm((2 * N, D), BF),
        vm((N, 4 * D), F32),
        vm((N, 2 * D), F32),
        vm((N, D), BF),
        vm((H, 2 * N, 2 * HD), BF),
        vm((H, N, 2 * HD), BF),
        vm((H, 2 * N, HD), BF),
        vm((N, WIN), F32),
        vm((N, HD), F32),
        vm((H, N, WIN), BF),
        vm((H, N, WIN), F32),
        vm((H, N, HD), F32),
        vm((N, D), BF),
        vm((H, N, HD), BF),
        vm((H, 2 * N, HD), F32),
        vm((H, 2 * N, HD), F32),
        vm((2, 2 * N, D), BF),
        vm((N, D), BF),
        vm((N, D), BF),
        vm((H, N, HD), F32),
        vm((N, D), BF),
        vm((N, D), BF),
        vm((NCH, 2, n_yx, rows, D), F32),
        vm((NCH, n_yx, rows, D), BF),
        vm((NCH, n_yx, rows, D), BF),
        vm((NCH, n_yx, rows, D), BF),
        vm((NCH, n_yx, rows, D), BF),
        vm((NCH, n_dp, rows, D), BF),
        vm((8, HD), F32),
        vm((8, HD), F32),
        vm((n_yx, 8, HD), F32),
        vm((n_dp, 8, HD), F32),
        dma((3,)),
        dma((3,)),
        dma((1,)),
        dma((1,)),
        dma((3, NCH)),
        dma((3, NCH)),
        dma((3,)),
        dma((3,)),
    ]
    spec = pl.BlockSpec(memory_space=pltpu.VMEM)
    lo, gi, gp, go, gt = pl.pallas_call(
        functools.partial(kernel, n_dp, n_seq),
        out_shape=(
            jax.ShapeDtypeStruct((N, D), BF),
            jax.ShapeDtypeStruct((N, D), BF),
            jax.ShapeDtypeStruct((rows, 4 * D), F32),
            jax.ShapeDtypeStruct((rows, D), F32),
            jax.ShapeDtypeStruct((H, HD // 2), F32),
        ),
        in_specs=[spec] * 8,
        out_specs=(spec,) * 5,
        scratch_shapes=scratch,
        compiler_params=pltpu.CompilerParams(
            collective_id=0, has_side_effects=True, vmem_limit_bytes=62 * 1024 * 1024
        ),
        name="layer",
    )(embeddings[0], user_ids, time_gaps, proj, out_w, freq2, mix2, cot[0])
    return lo[None], gi[None], gp, go, gt


def solution(mesh):
    n_dp, n_seq = mesh.shape["dp"], mesh.shape["seq"]
    return jax.shard_map(
        functools.partial(body, n_dp, n_seq),
        mesh=mesh,
        in_specs=(
            P("dp", "seq", None),
            P("dp", "seq"),
            P("dp", "seq"),
            P(),
            P(),
            P(),
            P(),
            P("dp", "seq", None),
        ),
        out_specs=(P("dp", "seq", None), P("dp", "seq", None), P("seq", None), P("seq", None), P()),
        check_vma=False,
    )
```

```python
import functools

import jax
import jax.numpy as jnp
from jax import lax
from jax.experimental import pallas as pl
from jax.experimental.pallas import tpu as pltpu
from jax.sharding import PartitionSpec as P

EPS = 1e-05
F32 = jnp.float32
BF = jnp.bfloat16
N = 512
D = 512
H = 4
HD = 128
TQ = 256
WIN = 768
MESH = pl.DeviceIdType.MESH


def nn(a, b):
    return lax.dot_general(a, b, (((1,), (0,)), ((), ())), preferred_element_type=F32)


def nt(a, b):
    return lax.dot_general(a, b, (((1,), (1,)), ((), ())), preferred_element_type=F32)


def tn(a, b):
    return lax.dot_general(a, b, (((0,), (0,)), ((), ())), preferred_element_type=F32)


def sigmoid(z):
    return 0.5 * jnp.tanh(0.5 * z) + 0.5


COS = (1.0, -1 / 2, 1 / 24, -1 / 720, 1 / 40320, -1 / 3628800, 1 / 479001600)
PI_PARTS = (3.140625, 9.67502593994140625e-4, 1.509957990978376432e-7)


def cos_sin(ang, half):
    k = jnp.floor(ang * (1.0 / 3.141592653589793) - half + 0.5)
    c = k + half
    r = ((ang - c * PI_PARTS[0]) - c * PI_PARTS[1]) - c * PI_PARTS[2]
    r2 = r * r
    p = jnp.full_like(r2, COS[-1])
    for q in COS[-2::-1]:
        p = p * r2 + q
    odd = k * 0.5
    odd = odd - jnp.floor(odd)
    return p * (1.0 - 4.0 * odd)


def kernel(n_dp, n_seq, names, *refs):
    r = dict(zip(names, refs))
    x_ref, u_ref, g_ref, w_ref, wo_ref, f_ref, mix_ref, cot_ref = refs[:8]
    lo_ref, gi_ref, gp_out, go_out, gt_out = refs[8:13]
    xv, xp, wv, wov, cotv = r["xv"], r["xp"], r["wv"], r["wov"], r["cotv"]
    uprev, gprev = r["uprev"], r["gprev"]
    nrm, nrmt, gatt = r["nrm"], r["nrmt"], r["gatt"]
    sl_v, sl_k, sl_q, sl_g = r["sl_v"], r["sl_k"], r["sl_q"], r["sl_g"]
    gate, kcat, qcat, v4 = r["gate"], r["kcat"], r["qcat"], r["v4"]
    maskf, cs_own, wsav, slp, att4 = r["maskf"], r["cs_own"], r["wsav"], r["slp"], r["att4"]
    ggs, ga4, gpv, gpk, gpq, gpg = r["ggs"], r["ga4"], r["gpv"], r["gpk"], r["gpq"], r["gpg"]
    back_s, back_r = r["back_s"], r["back_r"]
    t0_s, t0_r, t1_r, t2_r = r["t0_s"], r["t0_r"], r["t1_r"], r["t2_r"]
    in_sem, halo_ss, halo_rs = r["in_sem"], r["halo_ss"], r["halo_rs"]
    back_ss, back_rs, tm_ss, tm_rs = r["back_ss"], r["back_rs"], r["tm_ss"], r["tm_rs"]

    n_yx = n_seq // 2
    rows = D // n_seq
    half = D // 2
    dp = lax.axis_index("dp")
    s = lax.axis_index("seq")
    core = lax.rem(s, 2)
    m = lax.div(s, 2)
    right = lax.rem(s + 1, n_seq)
    left = lax.rem(s + n_seq - 1, n_seq)
    partner = m * 2 + 1 - core

    def yx_dev(i):
        return (dp, i * 2 + core)

    def z_dev(i):
        return (i, s)

    barrier = pltpu.get_barrier_semaphore()
    for peer in (left, right, partner):
        pl.semaphore_signal(barrier, inc=1, device_id=(dp, peer), device_id_type=MESH)

    @pl.loop(1, n_yx)
    def _(k):
        peer = lax.rem(m + k, n_yx)
        pl.semaphore_signal(barrier, inc=1, device_id=yx_dev(peer), device_id_type=MESH)

    @pl.loop(1, n_dp)
    def _(k):
        peer = lax.rem(dp + k, n_dp)
        pl.semaphore_signal(barrier, inc=1, device_id=z_dev(peer), device_id_type=MESH)

    loads = [
        pltpu.make_async_copy(x_ref, xv, in_sem.at[0]),
        pltpu.make_async_copy(w_ref, wv, in_sem.at[1]),
        pltpu.make_async_copy(wo_ref, wov, in_sem.at[2]),
        pltpu.make_async_copy(cot_ref, cotv, in_sem.at[3]),
    ]
    for copy in loads:
        copy.start()

    def remote(src, dst, ss, rs, dev):
        return pltpu.make_async_remote_copy(
            src_ref=src, dst_ref=dst, send_sem=ss, recv_sem=rs, device_id=dev, device_id_type=MESH
        )

    hi, lo = pl.ds(TQ, TQ), pl.ds(0, TQ)
    halo = [
        remote(u_ref, uprev, halo_ss.at[0], halo_rs.at[0], (dp, right)),
        remote(g_ref, gprev, halo_ss.at[1], halo_rs.at[1], (dp, right)),
        remote(xv.at[hi], xp.at[hi], halo_ss.at[2], halo_rs.at[2], (dp, right)),
        remote(xv.at[lo], xp.at[lo], halo_ss.at[3], halo_rs.at[3], (dp, right)),
    ]

    def norm(x):
        wide = x.astype(F32)
        scale = lax.rsqrt(jnp.mean(wide * wide, -1, keepdims=True) + EPS)
        return wide, scale

    def project(at, n, group):
        p = nn(nrm[at : at + n, :], wv[:, group * D : (group + 1) * D])
        sg = sigmoid(p)
        hid = p * sg
        return hid.astype(BF), sg + hid * (1.0 - sg)

    def put_heads(dst, at, val):
        n = val.shape[0]
        for h in range(H):
            dst[h, at : at + n, :HD] = val[:, h * HD : (h + 1) * HD]

    def put_kv(at, n):
        hid, sl = project(at, n, 1)
        put_heads(v4, at, hid)
        sl_v[at : at + n, :] = sl
        hid, sl = project(at, n, 3)
        put_heads(kcat, at, hid)
        sl_k[at : at + n, :] = sl

    def put_nrmt(at, n):
        t4 = jnp.transpose(nrm[at : at + n, :]).reshape(n_yx, 2, rows, n)
        for c in range(2):
            nrmt[c, :, at : at + n] = t4[:, c].reshape(half, n)

    loads[0].wait()
    wide, scale = norm(xv[...])
    nrm[N:, :] = (wide * scale).astype(BF)
    loads[1].wait()
    hid, sl = project(N, N, 0)
    gate[...] = hid
    sl_g[...] = sl

    pl.semaphore_wait(barrier, 3 + (n_yx - 1) + (n_dp - 1))
    for copy in halo:
        copy.start()

    put_kv(N, N)
    hid, sl = project(N, N, 2)
    put_heads(qcat, 0, hid)
    sl_q[...] = sl
    put_nrmt(N, N)
    loads[2].wait()
    loads[3].wait()
    ggs[...] = nt(cotv[...], wov[...])

    halo[0].wait_recv()
    halo[1].wait_recv()
    u_own = u_ref[...].astype(F32)
    u_prev = jnp.where(s == 0, -1.0, uprev[...].astype(F32))
    g_own = g_ref[...].astype(F32)
    g_prev = gprev[...].astype(F32)
    u_all = jnp.concatenate([u_prev, u_own], 1)
    g_all = jnp.broadcast_to(jnp.concatenate([g_prev, g_own], 1), (HD, 2 * N)).astype(BF)
    uc = jnp.transpose(jnp.broadcast_to(u_all, (HD, 2 * N)))[:, :1]
    freq = jnp.concatenate([f_ref[...], f_ref[...]], 1)
    mix = jnp.concatenate([mix_ref[...], mix_ref[...]], 1) * (HD**0.5)
    lane = lax.broadcasted_iota(jnp.int32, (1, HD), 1)
    shift = jnp.where(lane < HD // 2, 0.0, 0.5)

    def features(times):
        return cos_sin(times * freq, shift)

    for a in range(N // TQ):
        q0, k0 = a * TQ, a * TQ
        kpos = lax.broadcasted_iota(jnp.int32, (TQ, WIN), 1) + k0
        qpos = lax.broadcasted_iota(jnp.int32, (TQ, WIN), 0) + (q0 + N)
        same = uc[N + q0 : N + q0 + TQ, :] == u_all[:, k0 : k0 + WIN]
        mk = jnp.where(same & (kpos <= qpos), 1.0, 0.0)
        maskf[q0 : q0 + TQ, :] = mk
        feat = features(nt(mk.astype(BF), g_all[:, k0 : k0 + WIN]))
        cs_own[q0 : q0 + TQ, :] = feat
        fb = feat.astype(BF)
        for h in range(H):
            kcat[h, N + q0 : N + q0 + TQ, HD:] = fb
            qcat[h, q0 : q0 + TQ, HD:] = (feat * mix[h : h + 1, :]).astype(BF)
    pi = lax.broadcasted_iota(jnp.int32, (N, N), 0)
    pj = lax.broadcasted_iota(jnp.int32, (N, N), 1)
    mp = jnp.where((uc[:N, :] == u_all[:, :N]) & (pj <= pi), 1.0, 0.0).astype(BF)
    fb = features(nt(mp, g_all[:, :N])).astype(BF)
    for h in range(H):
        kcat[h, :N, HD:] = fb

    inv = HD**-0.5

    def piece(h, a, col, n):
        q0 = a * TQ
        k0 = q0 + col
        z = nt(qcat[h, q0 : q0 + TQ, :], kcat[h, k0 : k0 + n, :]) * inv
        sg = sigmoid(z) * maskf[q0 : q0 + TQ, col : col + n]
        wt = z * sg
        slp[h, q0 : q0 + TQ, col : col + n] = sg + wt * (1.0 - sg)
        wb = wt.astype(BF)
        wsav[h, q0 : q0 + TQ, col : col + n] = wb
        return nn(wb, v4[h, k0 : k0 + n, :])

    @pl.loop(0, H)
    def _(h):
        att4[h, :TQ, :] = piece(h, 0, N, TQ)
        att4[h, TQ:, :] = piece(h, 1, TQ, N)

    def halo_norm(at):
        wide, scale = norm(xp[at : at + TQ, :])
        nrm[at : at + TQ, :] = (wide * scale).astype(BF)
        put_kv(at, TQ)

    halo[2].wait_recv()
    halo_norm(TQ)

    @pl.loop(0, H)
    def _(h):
        att4[h, :TQ, :] += piece(h, 0, TQ, TQ)
        att4[h, TQ:, :] += piece(h, 1, 0, TQ)

    halo[3].wait_recv()
    halo_norm(0)

    @pl.loop(0, H)
    def _(h):
        att4[h, :TQ, :] += piece(h, 0, 0, TQ)

    attended = jnp.concatenate([att4[h] for h in range(H)], 1)
    scale_mid = lax.rsqrt(jnp.mean(attended * attended, -1, keepdims=True) + EPS)
    normed_mid = attended * scale_mid
    gate_wide = gate[...].astype(F32)
    gated = (normed_mid * gate_wide).astype(BF)
    t4 = jnp.transpose(gated).reshape(n_yx, 2, rows, N)
    for c in range(2):
        gatt[c] = t4[:, c].reshape(half, N)
    grad_gated = ggs[...]
    gpg[...] = (grad_gated * normed_mid * sl_g[...]).astype(BF)
    grad_mid = grad_gated * gate_wide
    ga = (
        scale_mid * (grad_mid - normed_mid * jnp.mean(grad_mid * normed_mid, -1, keepdims=True))
    ).astype(BF)
    for h in range(H):
        ga4[h] = ga[:, h * HD : (h + 1) * HD]

    def part(name, c):
        return r[c[0] + name].at[c[1]]

    def part_sem(name, c):
        i = c[1] + (0 if c[0] == "o" else 2)
        return lambda stage: r[name].at[stage, i]

    def stage_copy(stage, c, src, dst, dev):
        return remote(src, dst, part_sem("st_ss", c)(stage), part_sem("st_rs", c)(stage), dev)

    def s0_copy(c):
        return stage_copy(0, c, part("s0_s", c), part("s0_r", c), (dp, partner))

    def stage0(c, grad):
        width = 512 if c[0] == "o" else 3 * HD
        part("s0_s", c)[...] = grad(1 - core).reshape(n_yx, rows, width).astype(BF)
        s0_copy(c).start()
        part("own", c)[...] = grad(core).reshape(n_yx, rows, width)

    def stage1(c):
        s0_copy(c).wait_recv()
        s1_s, s1_r = part("s1_s", c), part("s1_r", c)
        s1_s[...] = (part("own", c)[...] + part("s0_r", c)[...].astype(F32)).astype(BF)
        s1_r[m] = s1_s[m]

        @pl.loop(1, n_yx)
        def _(k):
            peer = lax.rem(m + k, n_yx)
            stage_copy(1, c, s1_s.at[peer], s1_r.at[m], yx_dev(peer)).start()

    yx_part = pl.ds(0, n_yx - 1)
    z_part = pl.ds(0, n_dp - 1)

    def s1_all(c):
        ref = part("s1_r", c).at[yx_part]
        return stage_copy(1, c, ref, ref, (dp, partner))

    def z_all(c):
        ref = part("z_r", c).at[z_part]
        return stage_copy(2, c, ref, ref, (dp, partner))

    def stage2(c):
        s1_all(c).wait_recv()
        s1_r, z_r = part("s1_r", c), part("z_r", c)
        total = s1_r[0].astype(F32)
        for i in range(1, n_yx):
            total = total + s1_r[i].astype(F32)
        z_r[dp] = total.astype(BF)

        @pl.loop(1, n_dp)
        def _(k):
            peer = lax.rem(dp + k, n_dp)
            stage_copy(2, c, z_r.at[dp], z_r.at[dp], z_dev(peer)).start()

    factor = float(n_dp * n_seq * N) ** -0.5

    def stage3(c):
        z_all(c).wait_recv()
        z_r = part("z_r", c)
        total = z_r[0].astype(F32)
        for i in range(1, n_dp):
            total = total + z_r[i].astype(F32)
        total = total * factor
        if c == ("o", 0):
            go_out[...] = total
        elif c == ("o", 1):
            gp_out[:, :D] = total
        else:
            for i in range(3):
                at = (1 + i) * D + c[1] * HD
                gp_out[:, at : at + HD] = total[:, i * HD : (i + 1) * HD]

    out_c, gate_c = ("o", 0), ("o", 1)
    stage0(out_c, lambda c: nn(gatt[c], cotv[...]))
    stage0(gate_c, lambda c: nn(nrmt[c, :, N:], gpg[...]))
    put_nrmt(0, N)
    lo_ref[...] = (xv[...].astype(F32) + nn(gated, wov[...])).astype(BF)

    rowid = lax.broadcasted_iota(jnp.int32, (8, HD), 0)

    def head(h, tm):
        cols = slice(h * HD, (h + 1) * HD)
        tv, tk = [], []
        for a in range(N // TQ):
            q0, k0 = a * TQ, a * TQ
            gah = ga4[h, q0 : q0 + TQ, :]
            gw = nt(gah, v4[h, k0 : k0 + WIN, :])
            gs = (gw * slp[h, q0 : q0 + TQ, :]).astype(BF)
            tv.append(tn(wsav[h, q0 : q0 + TQ, :], gah))
            tk.append(tn(gs, qcat[h, q0 : q0 + TQ, :HD]))
            dqc = nn(gs, kcat[h, k0 : k0 + WIN, :])
            gpq[q0 : q0 + TQ, cols] = (dqc[:, :HD] * (sl_q[q0 : q0 + TQ, cols] * inv)).astype(BF)
            got = jnp.sum(dqc[:, HD:] * cs_own[q0 : q0 + TQ, :], 0, keepdims=True)
            tm = tm + jnp.where(rowid == h, got, 0.0)
        for dst, t, sl, f in ((gpv, tv, sl_v, 1.0), (gpk, tk, sl_k, inv)):
            dst[:TQ, cols] = (t[0][:TQ] * (sl[:TQ, cols] * f)).astype(BF)
            dst[TQ:WIN, cols] = ((t[0][TQ:] + t[1][:N]) * (sl[TQ:WIN, cols] * f)).astype(BF)
            dst[WIN:, cols] = (t[1][N:] * (sl[WIN:, cols] * f)).astype(BF)
        return tm

    def head_grad(h):
        cols = slice(h * HD, (h + 1) * HD)

        def grad(c):
            vk = nn(nrmt[c], jnp.concatenate([gpv[:, cols], gpk[:, cols]], 1))
            q = nn(nrmt[c, :, N:], gpq[:, cols])
            return jnp.concatenate([vk[:, :HD], q, vk[:, HD:]], 1)

        return grad

    hc = [("h", h) for h in range(H)]
    tm = head(0, jnp.zeros((8, HD), F32))
    stage1(out_c)
    stage0(hc[0], head_grad(0))
    tm = head(1, tm)
    stage1(gate_c)
    stage1(hc[0])
    stage0(hc[1], head_grad(1))
    tm = head(2, tm)
    stage1(hc[1])
    stage2(out_c)
    stage0(hc[2], head_grad(2))
    tm = head(3, tm)
    stage1(hc[2])
    stage2(gate_c)
    t0_s[...] = tm
    tm0 = remote(t0_s, t0_r, tm_ss.at[0], tm_rs.at[0], (dp, partner))
    tm0.start()
    stage0(hc[3], head_grad(3))
    back_s[...] = (nt(gpv[:N, :], wv[:, D : 2 * D]) + nt(gpk[:N, :], wv[:, 3 * D :])).astype(BF)
    stage2(hc[0])
    tm0.wait_recv()
    t1_r[m] = t0_s[...] + t0_r[...]

    @pl.loop(1, n_yx)
    def _(k):
        peer = lax.rem(m + k, n_yx)
        remote(t1_r.at[m], t1_r.at[m], tm_ss.at[1], tm_rs.at[1], yx_dev(peer)).start()

    stage1(hc[3])
    back = remote(back_s, back_r, back_ss.at[0], back_rs.at[0], (dp, left))
    back.start()
    stage2(hc[1])
    gn = (
        nt(gpg[...], wv[:, :D])
        + nt(gpv[N:, :], wv[:, D : 2 * D])
        + nt(gpq[...], wv[:, 2 * D : 3 * D])
        + nt(gpk[N:, :], wv[:, 3 * D :])
    )
    ggs[...] = gn

    def tm_all(ref, i):
        return remote(ref, ref, tm_ss.at[i], tm_rs.at[i], (dp, partner))

    tm1, tm2 = tm_all(t1_r.at[yx_part], 1), tm_all(t2_r.at[z_part], 2)
    tm1.wait_recv()
    tsum = t1_r[0]
    for i in range(1, n_yx):
        tsum = tsum + t1_r[i]
    t2_r[dp] = tsum

    @pl.loop(1, n_dp)
    def _(k):
        peer = lax.rem(dp + k, n_dp)
        remote(t2_r.at[dp], t2_r.at[dp], tm_ss.at[2], tm_rs.at[2], z_dev(peer)).start()

    stage2(hc[2])
    stage3(out_c)
    stage3(gate_c)
    stage2(hc[3])
    stage3(hc[0])
    back.wait_recv()
    wide, scale = norm(xv[...])
    unit = wide * scale
    gn = ggs[...] + back_r[...].astype(F32)
    gi_ref[...] = (
        cotv[...].astype(F32) + scale * (gn - unit * jnp.mean(gn * unit, -1, keepdims=True))
    ).astype(BF)
    stage3(hc[1])
    stage3(hc[2])
    tm2.wait_recv()
    tsum = t2_r[0]
    for i in range(1, n_dp):
        tsum = tsum + t2_r[i]
    tsum = (tsum + pltpu.roll(tsum, HD // 2, 1)) * factor
    gt_out[...] = tsum[:H, : HD // 2]
    stage3(hc[3])

    for copy in halo:
        copy.wait_send()
    back.wait_send()
    tm0.wait_send()
    tm1.wait_send()
    tm2.wait_send()
    for c in [out_c, gate_c] + hc:
        s0_copy(c).wait_send()
        s1_all(c).wait_send()
        z_all(c).wait_send()


def body(n_dp, n_seq, embeddings, user_ids, time_gaps, proj, out_w, freqs, mix, cot):
    n_yx = n_seq // 2
    rows = D // n_seq
    vm = pltpu.VMEM
    dma = pltpu.SemaphoreType.DMA
    scratch = {
        "xv": vm((N, D), BF),
        "xp": vm((N, D), BF),
        "wv": vm((D, 4 * D), BF),
        "wov": vm((D, D), BF),
        "cotv": vm((N, D), BF),
        "uprev": vm((1, N), jnp.int32),
        "gprev": vm((1, N), jnp.int32),
        "nrm": vm((2 * N, D), BF),
        "nrmt": vm((2, D // 2, 2 * N), BF),
        "gatt": vm((2, D // 2, N), BF),
        "sl_v": vm((2 * N, D), F32),
        "sl_k": vm((2 * N, D), F32),
        "sl_q": vm((N, D), F32),
        "sl_g": vm((N, D), F32),
        "gate": vm((N, D), BF),
        "kcat": vm((H, 2 * N, 2 * HD), BF),
        "qcat": vm((H, N, 2 * HD), BF),
        "v4": vm((H, 2 * N, HD), BF),
        "maskf": vm((N, WIN), F32),
        "cs_own": vm((N, HD), F32),
        "wsav": vm((H, N, WIN), BF),
        "slp": vm((H, N, WIN), F32),
        "att4": vm((H, N, HD), F32),
        "ggs": vm((N, D), F32),
        "ga4": vm((H, N, HD), BF),
        "gpv": vm((2 * N, D), BF),
        "gpk": vm((2 * N, D), BF),
        "gpq": vm((N, D), BF),
        "gpg": vm((N, D), BF),
        "back_s": vm((N, D), BF),
        "back_r": vm((N, D), BF),
        "t0_s": vm((8, HD), F32),
        "t0_r": vm((8, HD), F32),
        "t1_r": vm((n_yx, 8, HD), F32),
        "t2_r": vm((n_dp, 8, HD), F32),
        "in_sem": dma((4,)),
        "halo_ss": dma((4,)),
        "halo_rs": dma((4,)),
        "back_ss": dma((1,)),
        "back_rs": dma((1,)),
        "st_ss": dma((3, 2 + H)),
        "st_rs": dma((3, 2 + H)),
        "tm_ss": dma((3,)),
        "tm_rs": dma((3,)),
    }
    for kind, count, width in (("o", 2, D), ("h", H, 3 * HD)):
        for name in ("s0_s", "s0_r", "s1_s", "s1_r"):
            scratch[kind + name] = vm((count, n_yx, rows, width), BF)
        scratch[kind + "own"] = vm((count, n_yx, rows, width), F32)
        scratch[kind + "z_r"] = vm((count, n_dp, rows, width), BF)
    names = [str(i) for i in range(13)] + list(scratch)
    vspec = pl.BlockSpec(memory_space=pltpu.VMEM)
    hspec = pl.BlockSpec(memory_space=pltpu.HBM)
    lo, gi, gp, go, gt = pl.pallas_call(
        functools.partial(kernel, n_dp, n_seq, names),
        out_shape=(
            jax.ShapeDtypeStruct((N, D), BF),
            jax.ShapeDtypeStruct((N, D), BF),
            jax.ShapeDtypeStruct((rows, 4 * D), F32),
            jax.ShapeDtypeStruct((rows, D), F32),
            jax.ShapeDtypeStruct((H, HD // 2), F32),
        ),
        in_specs=[hspec, vspec, vspec, hspec, hspec, vspec, vspec, hspec],
        out_specs=(vspec,) * 5,
        scratch_shapes=list(scratch.values()),
        compiler_params=pltpu.CompilerParams(
            collective_id=0, has_side_effects=True, vmem_limit_bytes=56 * 1024 * 1024
        ),
        name="layer",
    )(embeddings[0], user_ids, time_gaps, proj, out_w, freqs[None], mix, cot[0])
    return lo[None], gi[None], gp, go, gt


def solution(mesh):
    n_dp, n_seq = mesh.shape["dp"], mesh.shape["seq"]
    return jax.shard_map(
        functools.partial(body, n_dp, n_seq),
        mesh=mesh,
        in_specs=(
            P("dp", "seq", None),
            P("dp", "seq"),
            P("dp", "seq"),
            P(),
            P(),
            P(),
            P(),
            P("dp", "seq", None),
        ),
        out_specs=(P("dp", "seq", None), P("dp", "seq", None), P("seq", None), P("seq", None), P()),
        check_vma=False,
    )
```

```python
import functools

import jax
import jax.numpy as jnp
from jax import lax
from jax.experimental import pallas as pl
from jax.experimental.pallas import tpu as pltpu
from jax.sharding import PartitionSpec as P

EPS = 1e-05
F32 = jnp.float32
BF = jnp.bfloat16
N = 512
D = 512
H = 4
HD = 128
TQ = 256
WIN = 768
MESH = pl.DeviceIdType.MESH


def nn(a, b):
    return lax.dot_general(a, b, (((1,), (0,)), ((), ())), preferred_element_type=F32)


def nt(a, b):
    return lax.dot_general(a, b, (((1,), (1,)), ((), ())), preferred_element_type=F32)


def tn(a, b):
    return lax.dot_general(a, b, (((0,), (0,)), ((), ())), preferred_element_type=F32)


def sigmoid(z):
    return 0.5 * jnp.tanh(0.5 * z) + 0.5


COS = (1.0, -1 / 2, 1 / 24, -1 / 720, 1 / 40320, -1 / 3628800, 1 / 479001600)
PI_PARTS = (3.140625, 9.67502593994140625e-4, 1.509957990978376432e-7)


def cos_sin(ang, half):
    k = jnp.floor(ang * (1.0 / 3.141592653589793) - half + 0.5)
    c = k + half
    r = ((ang - c * PI_PARTS[0]) - c * PI_PARTS[1]) - c * PI_PARTS[2]
    r2 = r * r
    p = jnp.full_like(r2, COS[-1])
    for q in COS[-2::-1]:
        p = p * r2 + q
    odd = k * 0.5
    odd = odd - jnp.floor(odd)
    return p * (1.0 - 4.0 * odd)


def kernel(n_dp, n_seq, names, *refs):
    r = dict(zip(names, refs))
    x_ref, u_ref, g_ref, w_ref, wo_ref, f_ref, mix_ref, cot_ref = refs[:8]
    lo_ref, gi_ref, gp_out, go_out, gt_out = refs[8:13]
    xv, xp, wv, wov, cotv = r["xv"], r["xp"], r["wv"], r["wov"], r["cotv"]
    uprev, gprev = r["uprev"], r["gprev"]
    nrm, nrmt, gatt = r["nrm"], r["nrmt"], r["gatt"]
    sl_v, sl_k, sl_q, sl_g = r["sl_v"], r["sl_k"], r["sl_q"], r["sl_g"]
    gate, kcat, qcat, v4 = r["gate"], r["kcat"], r["qcat"], r["v4"]
    maskf, cs_own, wsav, slp, att4 = r["maskf"], r["cs_own"], r["wsav"], r["slp"], r["att4"]
    ggs, ga4, gpv, gpk, gpq, gpg = r["ggs"], r["ga4"], r["gpv"], r["gpk"], r["gpq"], r["gpg"]
    back_s, back_r, gated_s = r["back_s"], r["back_r"], r["gated_s"]
    t0_s, t0_r, t1_r, t2_r = r["t0_s"], r["t0_r"], r["t1_r"], r["t2_r"]
    in_sem, halo_ss, halo_rs = r["in_sem"], r["halo_ss"], r["halo_rs"]
    back_ss, back_rs, tm_ss, tm_rs = r["back_ss"], r["back_rs"], r["tm_ss"], r["tm_rs"]

    n_yx = n_seq // 2
    rows = D // n_seq
    half = D // 2
    dp = lax.axis_index("dp")
    s = lax.axis_index("seq")
    core = lax.rem(s, 2)
    m = lax.div(s, 2)
    right = lax.rem(s + 1, n_seq)
    left = lax.rem(s + n_seq - 1, n_seq)
    partner = m * 2 + 1 - core

    def yx_dev(i):
        return (dp, i * 2 + core)

    def z_dev(i):
        return (i, s)

    barrier = pltpu.get_barrier_semaphore()
    for peer in (left, right, partner):
        pl.semaphore_signal(barrier, inc=1, device_id=(dp, peer), device_id_type=MESH)

    @pl.loop(1, n_yx)
    def _(k):
        peer = lax.rem(m + k, n_yx)
        pl.semaphore_signal(barrier, inc=1, device_id=yx_dev(peer), device_id_type=MESH)

    @pl.loop(1, n_dp)
    def _(k):
        peer = lax.rem(dp + k, n_dp)
        pl.semaphore_signal(barrier, inc=1, device_id=z_dev(peer), device_id_type=MESH)

    loads = [
        pltpu.make_async_copy(x_ref, xv, in_sem.at[0]),
        pltpu.make_async_copy(w_ref, wv, in_sem.at[1]),
        pltpu.make_async_copy(wo_ref, wov, in_sem.at[2]),
        pltpu.make_async_copy(cot_ref, cotv, in_sem.at[3]),
    ]
    for copy in loads:
        copy.start()

    def remote(src, dst, ss, rs, dev):
        return pltpu.make_async_remote_copy(
            src_ref=src, dst_ref=dst, send_sem=ss, recv_sem=rs, device_id=dev, device_id_type=MESH
        )

    hi, lo = pl.ds(TQ, TQ), pl.ds(0, TQ)
    halo = [
        remote(u_ref, uprev, halo_ss.at[0], halo_rs.at[0], (dp, right)),
        remote(g_ref, gprev, halo_ss.at[1], halo_rs.at[1], (dp, right)),
        remote(xv.at[hi], xp.at[hi], halo_ss.at[2], halo_rs.at[2], (dp, right)),
        remote(xv.at[lo], xp.at[lo], halo_ss.at[3], halo_rs.at[3], (dp, right)),
    ]

    def norm(x):
        wide = x.astype(F32)
        scale = lax.rsqrt(jnp.mean(wide * wide, -1, keepdims=True) + EPS)
        return wide, scale

    def project(at, n, group):
        p = nn(nrm[at : at + n, :], wv[:, group * D : (group + 1) * D])
        sg = sigmoid(p)
        hid = p * sg
        return hid.astype(BF), sg + hid * (1.0 - sg)

    def put_heads(dst, at, val):
        n = val.shape[0]
        for h in range(H):
            dst[h, at : at + n, :HD] = val[:, h * HD : (h + 1) * HD]

    def put_kv(at, n):
        hid, sl = project(at, n, 1)
        put_heads(v4, at, hid)
        sl_v[at : at + n, :] = sl
        hid, sl = project(at, n, 3)
        put_heads(kcat, at, hid)
        sl_k[at : at + n, :] = sl

    def put_nrmt(at, n):
        t4 = jnp.transpose(nrm[at : at + n, :]).reshape(n_yx, 2, rows, n)
        for c in range(2):
            nrmt[c, :, at : at + n] = t4[:, c].reshape(half, n)

    loads[0].wait()
    wide, scale = norm(xv[...])
    nrm[N:, :] = (wide * scale).astype(BF)
    loads[1].wait()
    hid, sl = project(N, N, 0)
    gate[...] = hid
    sl_g[...] = sl

    pl.semaphore_wait(barrier, 3 + (n_yx - 1) + (n_dp - 1))
    for copy in halo:
        copy.start()

    put_kv(N, N)
    hid, sl = project(N, N, 2)
    put_heads(qcat, 0, hid)
    sl_q[...] = sl
    put_nrmt(N, N)
    loads[2].wait()
    loads[3].wait()
    ggs[...] = nt(cotv[...], wov[...])

    halo[0].wait_recv()
    halo[1].wait_recv()
    u_own = u_ref[...].astype(F32)
    u_prev = jnp.where(s == 0, -1.0, uprev[...].astype(F32))
    g_own = g_ref[...].astype(F32)
    g_prev = gprev[...].astype(F32)
    u_all = jnp.concatenate([u_prev, u_own], 1)
    g_all = jnp.broadcast_to(jnp.concatenate([g_prev, g_own], 1), (HD, 2 * N)).astype(BF)
    uc = jnp.transpose(jnp.broadcast_to(u_all, (HD, 2 * N)))[:, :1]
    freq = jnp.concatenate([f_ref[...], f_ref[...]], 1)
    mix = jnp.concatenate([mix_ref[...], mix_ref[...]], 1) * (HD**0.5)
    lane = lax.broadcasted_iota(jnp.int32, (1, HD), 1)
    shift = jnp.where(lane < HD // 2, 0.0, 0.5)

    def features(times):
        return cos_sin(times * freq, shift)

    for a in range(N // TQ):
        q0, k0 = a * TQ, a * TQ
        kpos = lax.broadcasted_iota(jnp.int32, (TQ, WIN), 1) + k0
        qpos = lax.broadcasted_iota(jnp.int32, (TQ, WIN), 0) + (q0 + N)
        same = uc[N + q0 : N + q0 + TQ, :] == u_all[:, k0 : k0 + WIN]
        mk = jnp.where(same & (kpos <= qpos), 1.0, 0.0)
        maskf[q0 : q0 + TQ, :] = mk
        feat = features(nt(mk.astype(BF), g_all[:, k0 : k0 + WIN]))
        cs_own[q0 : q0 + TQ, :] = feat
        fb = feat.astype(BF)
        for h in range(H):
            kcat[h, N + q0 : N + q0 + TQ, HD:] = fb
            qcat[h, q0 : q0 + TQ, HD:] = (feat * mix[h : h + 1, :]).astype(BF)
    pi = lax.broadcasted_iota(jnp.int32, (N, N), 0)
    pj = lax.broadcasted_iota(jnp.int32, (N, N), 1)
    mp = jnp.where((uc[:N, :] == u_all[:, :N]) & (pj <= pi), 1.0, 0.0).astype(BF)
    fb = features(nt(mp, g_all[:, :N])).astype(BF)
    for h in range(H):
        kcat[h, :N, HD:] = fb

    inv = HD**-0.5

    def piece(h, a, col, n):
        q0 = a * TQ
        k0 = q0 + col
        z = nt(qcat[h, q0 : q0 + TQ, :], kcat[h, k0 : k0 + n, :]) * inv
        sg = sigmoid(z) * maskf[q0 : q0 + TQ, col : col + n]
        wt = z * sg
        slp[h, q0 : q0 + TQ, col : col + n] = sg + wt * (1.0 - sg)
        wb = wt.astype(BF)
        wsav[h, q0 : q0 + TQ, col : col + n] = wb
        return nn(wb, v4[h, k0 : k0 + n, :])

    @pl.loop(0, H)
    def _(h):
        att4[h, :TQ, :] = piece(h, 0, N, TQ)
        att4[h, TQ:, :] = piece(h, 1, TQ, N)

    def halo_norm(at):
        wide, scale = norm(xp[at : at + TQ, :])
        nrm[at : at + TQ, :] = (wide * scale).astype(BF)
        put_kv(at, TQ)

    halo[2].wait_recv()
    halo_norm(TQ)

    @pl.loop(0, H)
    def _(h):
        att4[h, :TQ, :] += piece(h, 0, TQ, TQ)
        att4[h, TQ:, :] += piece(h, 1, 0, TQ)

    halo[3].wait_recv()
    halo_norm(0)

    @pl.loop(0, H)
    def _(h):
        att4[h, :TQ, :] += piece(h, 0, 0, TQ)

    attended = jnp.concatenate([att4[h] for h in range(H)], 1)
    scale_mid = lax.rsqrt(jnp.mean(attended * attended, -1, keepdims=True) + EPS)
    normed_mid = attended * scale_mid
    gate_wide = gate[...].astype(F32)
    gated = (normed_mid * gate_wide).astype(BF)
    gated_s[...] = gated
    t4 = jnp.transpose(gated).reshape(n_yx, 2, rows, N)
    for c in range(2):
        gatt[c] = t4[:, c].reshape(half, N)
    grad_gated = ggs[...]
    gpg[...] = (grad_gated * normed_mid * sl_g[...]).astype(BF)
    grad_mid = grad_gated * gate_wide
    ga = (
        scale_mid * (grad_mid - normed_mid * jnp.mean(grad_mid * normed_mid, -1, keepdims=True))
    ).astype(BF)
    for h in range(H):
        ga4[h] = ga[:, h * HD : (h + 1) * HD]

    w_h = 2 * HD
    tiles = (rows // 8) * (D // HD)
    per = tiles // n_dp

    def part(name, c):
        return r[c[0] + name].at[c[1]]

    def stage_copy(stage, c, src, dst, dev):
        i = c[1] + (0 if c[0] == "o" else 3)
        return remote(src, dst, r["st_ss"].at[stage, i], r["st_rs"].at[stage, i], dev)

    def whole(stage, c, ref):
        return stage_copy(stage, c, ref, ref, (dp, partner))

    waits = []

    def spread(stage, c, n, me, send):
        @pl.loop(1, n)
        def _(k):
            peer = lax.rem(me + k, n)
            src, dst, dev = send(peer)
            stage_copy(stage, c, src, dst, dev).start()

    def received(stage, c, ref, n):
        copy = whole(stage, c, ref.at[pl.ds(0, n - 1)])
        copy.wait_recv()
        waits.append(copy)

    def total_of(ref, n):
        total = ref[0].astype(F32)
        for i in range(1, n):
            total = total + ref[i].astype(F32)
        return total

    def s0_copy(c):
        return stage_copy(0, c, part("s0_s", c), part("s0_r", c), (dp, partner))

    def stage0(c, grad):
        shape = (n_yx, rows, D if c[0] == "o" else w_h)
        part("s0_s", c)[...] = grad(1 - core).reshape(shape).astype(BF)
        s0_copy(c).start()
        part("own", c)[...] = grad(core).reshape(shape)

    def pair_sum(c):
        copy = s0_copy(c)
        copy.wait_recv()
        waits.append(copy)
        return (part("own", c)[...] + part("s0_r", c)[...].astype(F32)).astype(BF)

    def h1(c):
        s_ref, r_ref = part("s1_s", c), part("s1_r", c)
        s_ref[...] = pair_sum(c)
        r_ref[m] = s_ref[m]
        spread(1, c, n_yx, m, lambda p: (s_ref.at[p], r_ref.at[m], yx_dev(p)))

    def o3(c):
        s_ref, r_ref = part("z_s", c), part("z_r", c)
        received(1, c, part("s1_r", c), n_yx)
        total = total_of(part("s1_r", c), n_yx).astype(BF)
        for i in range(tiles):
            at, col = i // (D // HD) * 8, i % (D // HD) * HD
            s_ref[i // per, i % per] = total[at : at + 8, col : col + HD]
        r_ref[dp] = s_ref[dp]
        spread(3, c, n_dp, dp, lambda p: (s_ref.at[p], r_ref.at[dp], z_dev(p)))

    def o4(c):
        r_ref = part("g_r", c)
        received(3, c, part("z_r", c), n_dp)
        r_ref[dp] = total_of(part("z_r", c), n_dp).astype(BF)
        spread(4, c, n_dp, dp, lambda p: (r_ref.at[dp], r_ref.at[dp], z_dev(p)))

    factor = float(n_dp * n_seq * N) ** -0.5

    def o5(c):
        r_ref = part("g_r", c)
        received(4, c, r_ref, n_dp)
        for i in range(tiles):
            at, col = i // (D // HD) * 8, i % (D // HD) * HD
            tile = r_ref[i // per, i % per].astype(F32) * factor
            if c[1] == 0:
                go_out[at : at + 8, col : col + HD] = tile
            else:
                base = (c[1] - 1) * D + col
                gp_out[at : at + 8, base : base + HD] = tile

    def h2(c):
        r_ref = part("z_r", c)
        received(1, c, part("s1_r", c), n_yx)
        r_ref[dp] = total_of(part("s1_r", c), n_yx).astype(BF)
        spread(2, c, n_dp, dp, lambda p: (r_ref.at[dp], r_ref.at[dp], z_dev(p)))

    def h3(c):
        received(2, c, part("z_r", c), n_dp)
        total = total_of(part("z_r", c), n_dp) * factor
        gp_out[:, 2 * D + c[1] * HD : 2 * D + (c[1] + 1) * HD] = total[:, :HD]
        gp_out[:, 3 * D + c[1] * HD : 3 * D + (c[1] + 1) * HD] = total[:, HD:]

    out_c, gate_c, val_c = ("o", 0), ("o", 1), ("o", 2)
    hc = [("h", h) for h in range(H)]
    stage0(out_c, lambda c: nn(gatt[c], cotv[...]))
    stage0(gate_c, lambda c: nn(nrmt[c, :, N:], gpg[...]))
    put_nrmt(0, N)

    def put_window(dst, t, sl, f, cols):
        dst[:TQ, cols] = (t[0][:TQ] * (sl[:TQ, cols] * f)).astype(BF)
        dst[TQ:WIN, cols] = ((t[0][TQ:] + t[1][:N]) * (sl[TQ:WIN, cols] * f)).astype(BF)
        dst[WIN:, cols] = (t[1][N:] * (sl[WIN:, cols] * f)).astype(BF)

    for h in range(H):
        t = [
            tn(wsav[h, q0 : q0 + TQ, :], ga4[h, q0 : q0 + TQ, :]) for q0 in range(0, N, TQ)
        ]
        put_window(gpv, t, sl_v, 1.0, slice(h * HD, (h + 1) * HD))
    h1(out_c)
    stage0(val_c, lambda c: nn(nrmt[c], gpv[...]))

    rowid = lax.broadcasted_iota(jnp.int32, (8, HD), 0)

    def head(h, tm, *between):
        cols = slice(h * HD, (h + 1) * HD)
        tk = []
        for a in range(N // TQ):
            q0, k0 = a * TQ, a * TQ
            gw = nt(ga4[h, q0 : q0 + TQ, :], v4[h, k0 : k0 + WIN, :])
            gs = (gw * slp[h, q0 : q0 + TQ, :]).astype(BF)
            tk.append(tn(gs, qcat[h, q0 : q0 + TQ, :HD]))
            dqc = nn(gs, kcat[h, k0 : k0 + WIN, :])
            gpq[q0 : q0 + TQ, cols] = (dqc[:, :HD] * (sl_q[q0 : q0 + TQ, cols] * inv)).astype(BF)
            got = jnp.sum(dqc[:, HD:] * cs_own[q0 : q0 + TQ, :], 0, keepdims=True)
            tm = tm + jnp.where(rowid == h, got, 0.0)
            if a == 0:
                for step, c in between:
                    step(c)
        put_window(gpk, tk, sl_k, inv, cols)
        return tm

    def head_grad(h):
        cols = slice(h * HD, (h + 1) * HD)

        def grad(c):
            own = nn(nrmt[c, :, N:], jnp.concatenate([gpq[:, cols], gpk[N:, cols]], 1))
            prev = nn(nrmt[c, :, :N], gpk[:N, cols])
            return jnp.concatenate([own[:, :HD], own[:, HD:] + prev], 1)

        return grad

    tm = head(0, jnp.zeros((8, HD), F32), (h1, gate_c))
    h1(val_c)
    stage0(hc[0], head_grad(0))
    tm = head(1, tm)
    h1(hc[0])
    stage0(hc[1], head_grad(1))
    tm = head(2, tm)
    h1(hc[1])
    stage0(hc[2], head_grad(2))
    tm = head(3, tm, (o3, out_c))
    h1(hc[2])
    t0_s[...] = tm
    tm0 = remote(t0_s, t0_r, tm_ss.at[0], tm_rs.at[0], (dp, partner))
    tm0.start()
    stage0(hc[3], head_grad(3))
    o3(gate_c)
    back_s[...] = (nt(gpv[:N, :], wv[:, D : 2 * D]) + nt(gpk[:N, :], wv[:, 3 * D :])).astype(BF)
    h1(hc[3])
    tm0.wait_recv()
    t1_r[m] = t0_s[...] + t0_r[...]

    @pl.loop(1, n_yx)
    def _(k):
        peer = lax.rem(m + k, n_yx)
        remote(t1_r.at[m], t1_r.at[m], tm_ss.at[1], tm_rs.at[1], yx_dev(peer)).start()

    back = remote(back_s, back_r, back_ss.at[0], back_rs.at[0], (dp, left))
    back.start()
    o3(val_c)
    h2(hc[0])
    lo_ref[...] = (xv[...].astype(F32) + nn(gated_s[...], wov[...])).astype(BF)
    ggs[...] = (
        nt(gpg[...], wv[:, :D])
        + nt(gpv[N:, :], wv[:, D : 2 * D])
        + nt(gpq[...], wv[:, 2 * D : 3 * D])
        + nt(gpk[N:, :], wv[:, 3 * D :])
    )
    h2(hc[1])
    o4(out_c)
    h2(hc[2])
    o4(gate_c)

    def tm_all(ref, i):
        return remote(ref, ref, tm_ss.at[i], tm_rs.at[i], (dp, partner))

    tm1, tm2 = tm_all(t1_r.at[pl.ds(0, n_yx - 1)], 1), tm_all(t2_r.at[pl.ds(0, n_dp - 1)], 2)
    tm1.wait_recv()
    tsum = t1_r[0]
    for i in range(1, n_yx):
        tsum = tsum + t1_r[i]
    t2_r[dp] = tsum

    @pl.loop(1, n_dp)
    def _(k):
        peer = lax.rem(dp + k, n_dp)
        remote(t2_r.at[dp], t2_r.at[dp], tm_ss.at[2], tm_rs.at[2], z_dev(peer)).start()

    o4(val_c)
    h2(hc[3])
    back.wait_recv()
    wide, scale = norm(xv[...])
    unit = wide * scale
    gn = ggs[...] + back_r[...].astype(F32)
    gi_ref[...] = (
        cotv[...].astype(F32) + scale * (gn - unit * jnp.mean(gn * unit, -1, keepdims=True))
    ).astype(BF)
    h3(hc[0])
    h3(hc[1])
    h3(hc[2])
    o5(out_c)
    o5(gate_c)
    o5(val_c)
    tm2.wait_recv()
    tsum = t2_r[0]
    for i in range(1, n_dp):
        tsum = tsum + t2_r[i]
    tsum = (tsum + pltpu.roll(tsum, HD // 2, 1)) * factor
    gt_out[...] = tsum[:H, : HD // 2]
    h3(hc[3])

    for copy in halo + [back, tm0, tm1, tm2] + waits:
        copy.wait_send()


def store(*refs):
    sems = refs[10]
    copies = [pltpu.make_async_copy(refs[i], refs[5 + i], sems.at[i]) for i in range(5)]
    for copy in copies:
        copy.start()
    for copy in copies:
        copy.wait()


def body(n_dp, n_seq, embeddings, user_ids, time_gaps, proj, out_w, freqs, mix, cot):
    n_yx = n_seq // 2
    rows = D // n_seq
    vm = pltpu.VMEM
    dma = pltpu.SemaphoreType.DMA
    scratch = {
        "xv": vm((N, D), BF),
        "xp": vm((N, D), BF),
        "wv": vm((D, 4 * D), BF),
        "wov": vm((D, D), BF),
        "cotv": vm((N, D), BF),
        "uprev": vm((1, N), jnp.int32),
        "gprev": vm((1, N), jnp.int32),
        "nrm": vm((2 * N, D), BF),
        "nrmt": vm((2, D // 2, 2 * N), BF),
        "gatt": vm((2, D // 2, N), BF),
        "sl_v": vm((2 * N, D), F32),
        "sl_k": vm((2 * N, D), F32),
        "sl_q": vm((N, D), F32),
        "sl_g": vm((N, D), F32),
        "gate": vm((N, D), BF),
        "kcat": vm((H, 2 * N, 2 * HD), BF),
        "qcat": vm((H, N, 2 * HD), BF),
        "v4": vm((H, 2 * N, HD), BF),
        "maskf": vm((N, WIN), F32),
        "cs_own": vm((N, HD), F32),
        "wsav": vm((H, N, WIN), BF),
        "slp": vm((H, N, WIN), F32),
        "att4": vm((H, N, HD), F32),
        "ggs": vm((N, D), F32),
        "ga4": vm((H, N, HD), BF),
        "gpv": vm((2 * N, D), BF),
        "gpk": vm((2 * N, D), BF),
        "gpq": vm((N, D), BF),
        "gpg": vm((N, D), BF),
        "gated_s": vm((N, D), BF),
        "back_s": vm((N, D), BF),
        "back_r": vm((N, D), BF),
        "t0_s": vm((8, HD), F32),
        "t0_r": vm((8, HD), F32),
        "t1_r": vm((n_yx, 8, HD), F32),
        "t2_r": vm((n_dp, 8, HD), F32),
        "in_sem": dma((4,)),
        "halo_ss": dma((4,)),
        "halo_rs": dma((4,)),
        "back_ss": dma((1,)),
        "back_rs": dma((1,)),
        "st_ss": dma((5, 3 + H)),
        "st_rs": dma((5, 3 + H)),
        "tm_ss": dma((3,)),
        "tm_rs": dma((3,)),
    }
    per = (rows // 8) * (D // HD) // n_dp
    for kind, count, width in (("o", 3, D), ("h", H, 2 * HD)):
        for name in ("s0_s", "s0_r", "s1_s", "s1_r"):
            scratch[kind + name] = vm((count, n_yx, rows, width), BF)
        scratch[kind + "own"] = vm((count, n_yx, rows, width), F32)
    for name in ("z_s", "z_r", "g_r"):
        scratch["o" + name] = vm((3, n_dp, per, 8, HD), BF)
    scratch["hz_r"] = vm((H, n_dp, rows, 2 * HD), BF)
    names = [str(i) for i in range(13)] + list(scratch)
    vspec = pl.BlockSpec(memory_space=pltpu.VMEM)
    hspec = pl.BlockSpec(memory_space=pltpu.HBM)
    results = (
        ((N, D), BF),
        ((N, D), BF),
        ((rows, 4 * D), F32),
        ((rows, D), F32),
        ((H, HD // 2), F32),
    )
    held = pl.pallas_call(
        functools.partial(kernel, n_dp, n_seq, names),
        out_shape=tuple(vm(shape, dtype) for shape, dtype in results),
        in_specs=[hspec, vspec, vspec, hspec, hspec, vspec, vspec, hspec],
        out_specs=(vspec,) * 5,
        scratch_shapes=list(scratch.values()),
        compiler_params=pltpu.CompilerParams(
            collective_id=0, has_side_effects=True, vmem_limit_bytes=56 * 1024 * 1024
        ),
        name="layer",
    )(embeddings[0], user_ids, time_gaps, proj, out_w, freqs[None], mix, cot[0])
    lo, gi, gp, go, gt = pl.pallas_call(
        store,
        out_shape=tuple(jax.ShapeDtypeStruct(shape, dtype) for shape, dtype in results),
        in_specs=[vspec] * 5,
        out_specs=(hspec,) * 5,
        scratch_shapes=[dma((5,))],
        compiler_params=pltpu.CompilerParams(vmem_limit_bytes=4 * 1024 * 1024),
        name="store",
    )(*held)
    return lo[None], gi[None], gp, go, gt


def solution(mesh):
    n_dp, n_seq = mesh.shape["dp"], mesh.shape["seq"]
    return jax.shard_map(
        functools.partial(body, n_dp, n_seq),
        mesh=mesh,
        in_specs=(
            P("dp", "seq", None),
            P("dp", "seq"),
            P("dp", "seq"),
            P(),
            P(),
            P(),
            P(),
            P("dp", "seq", None),
        ),
        out_specs=(P("dp", "seq", None), P("dp", "seq", None), P("seq", None), P("seq", None), P()),
        check_vma=False,
    )
```

```python
import functools

import jax
import jax.numpy as jnp
from jax import lax
from jax.experimental import pallas as pl
from jax.experimental.pallas import tpu as pltpu
from jax.sharding import PartitionSpec as P

EPS = 1e-05
F32 = jnp.float32
BF = jnp.bfloat16
N = 512
D = 512
H = 4
HD = 128
TQ = 256
WIN = 768
MESH = pl.DeviceIdType.MESH


def nn(a, b):
    return lax.dot_general(a, b, (((1,), (0,)), ((), ())), preferred_element_type=F32)


def nt(a, b):
    return lax.dot_general(a, b, (((1,), (1,)), ((), ())), preferred_element_type=F32)


def tn(a, b):
    return lax.dot_general(a, b, (((0,), (0,)), ((), ())), preferred_element_type=F32)


def sigmoid(z):
    return 0.5 * jnp.tanh(0.5 * z) + 0.5


COS = (1.0, -1 / 2, 1 / 24, -1 / 720, 1 / 40320, -1 / 3628800, 1 / 479001600)
PI_PARTS = (3.140625, 9.67502593994140625e-4, 1.509957990978376432e-7)


def cos_sin(ang, half):
    k = jnp.floor(ang * (1.0 / 3.141592653589793) - half + 0.5)
    c = k + half
    r = ((ang - c * PI_PARTS[0]) - c * PI_PARTS[1]) - c * PI_PARTS[2]
    r2 = r * r
    p = jnp.full_like(r2, COS[-1])
    for q in COS[-2::-1]:
        p = p * r2 + q
    odd = k * 0.5
    odd = odd - jnp.floor(odd)
    return p * (1.0 - 4.0 * odd)


def kernel(n_dp, n_seq, names, *refs):
    r = dict(zip(names, refs))
    x_ref, u_ref, g_ref, w_ref, wo_ref, f_ref, mix_ref, cot_ref = refs[:8]
    lo_ref, gi_ref, gp_out, go_out, gt_out = refs[8:13]
    xv, xp, wv, wov, cotv = r["xv"], r["xp"], r["wv"], r["wov"], r["cotv"]
    uprev, gprev = r["uprev"], r["gprev"]
    nrm, nrmt, gatt = r["nrm"], r["nrmt"], r["gatt"]
    sl_v, sl_k, sl_q, sl_g = r["sl_v"], r["sl_k"], r["sl_q"], r["sl_g"]
    gate, kcat, qcat, v4 = r["gate"], r["kcat"], r["qcat"], r["v4"]
    maskf, cs_own, wsav, slp, att4 = r["maskf"], r["cs_own"], r["wsav"], r["slp"], r["att4"]
    ggs, ga4, gpv, gpk, gpq, gpg = r["ggs"], r["ga4"], r["gpv"], r["gpk"], r["gpq"], r["gpg"]
    back_s, back_r, gated_s = r["back_s"], r["back_r"], r["gated_s"]
    t0_s, t0_r, t1_r, t2_r = r["t0_s"], r["t0_r"], r["t1_r"], r["t2_r"]
    in_sem, halo_ss, halo_rs = r["in_sem"], r["halo_ss"], r["halo_rs"]
    back_ss, back_rs, tm_ss, tm_rs = r["back_ss"], r["back_rs"], r["tm_ss"], r["tm_rs"]

    n_yx = n_seq // 2
    rows = D // n_seq
    half = D // 2
    dp = lax.axis_index("dp")
    s = lax.axis_index("seq")
    core = lax.rem(s, 2)
    m = lax.div(s, 2)
    right = lax.rem(s + 1, n_seq)
    left = lax.rem(s + n_seq - 1, n_seq)
    partner = m * 2 + 1 - core

    def yx_dev(i):
        return (dp, i * 2 + core)

    def z_dev(i):
        return (i, s)

    barrier = pltpu.get_barrier_semaphore()
    for peer in (left, right, partner):
        pl.semaphore_signal(barrier, inc=1, device_id=(dp, peer), device_id_type=MESH)

    @pl.loop(1, n_yx)
    def _(k):
        peer = lax.rem(m + k, n_yx)
        pl.semaphore_signal(barrier, inc=1, device_id=yx_dev(peer), device_id_type=MESH)

    @pl.loop(1, n_dp)
    def _(k):
        peer = lax.rem(dp + k, n_dp)
        pl.semaphore_signal(barrier, inc=1, device_id=z_dev(peer), device_id_type=MESH)

    loads = [
        pltpu.make_async_copy(x_ref, xv, in_sem.at[0]),
        pltpu.make_async_copy(w_ref, wv, in_sem.at[1]),
        pltpu.make_async_copy(wo_ref, wov, in_sem.at[2]),
        pltpu.make_async_copy(cot_ref, cotv, in_sem.at[3]),
        pltpu.make_async_copy(u_ref, r["uv"], in_sem.at[4]),
        pltpu.make_async_copy(g_ref, r["gv"], in_sem.at[5]),
        pltpu.make_async_copy(f_ref, r["fv"], in_sem.at[6]),
        pltpu.make_async_copy(mix_ref, r["mv"], in_sem.at[7]),
    ]
    for copy in loads:
        copy.start()

    def remote(src, dst, ss, rs, dev):
        return pltpu.make_async_remote_copy(
            src_ref=src, dst_ref=dst, send_sem=ss, recv_sem=rs, device_id=dev, device_id_type=MESH
        )

    hi, lo = pl.ds(TQ, TQ), pl.ds(0, TQ)
    halo = [
        remote(r["uv"], uprev, halo_ss.at[0], halo_rs.at[0], (dp, right)),
        remote(r["gv"], gprev, halo_ss.at[1], halo_rs.at[1], (dp, right)),
        remote(xv.at[hi], xp.at[hi], halo_ss.at[2], halo_rs.at[2], (dp, right)),
        remote(xv.at[lo], xp.at[lo], halo_ss.at[3], halo_rs.at[3], (dp, right)),
    ]

    def norm(x):
        wide = x.astype(F32)
        scale = lax.rsqrt(jnp.mean(wide * wide, -1, keepdims=True) + EPS)
        return wide, scale

    def project(at, n, group):
        p = nn(nrm[at : at + n, :], wv[:, group * D : (group + 1) * D])
        sg = sigmoid(p)
        hid = p * sg
        return hid.astype(BF), sg + hid * (1.0 - sg)

    def put_heads(dst, at, val):
        n = val.shape[0]
        for h in range(H):
            dst[h, at : at + n, :HD] = val[:, h * HD : (h + 1) * HD]

    def put_kv(at, n):
        hid, sl = project(at, n, 1)
        put_heads(v4, at, hid)
        sl_v[at : at + n, :] = sl
        hid, sl = project(at, n, 3)
        put_heads(kcat, at, hid)
        sl_k[at : at + n, :] = sl

    def put_nrmt(at, n):
        t4 = jnp.transpose(nrm[at : at + n, :]).reshape(n_yx, 2, rows, n)
        for c in range(2):
            nrmt[c, :, at : at + n] = t4[:, c].reshape(half, n)

    loads[0].wait()
    wide, scale = norm(xv[...])
    nrm[N:, :] = (wide * scale).astype(BF)
    loads[1].wait()
    hid, sl = project(N, N, 0)
    gate[...] = hid
    sl_g[...] = sl

    for copy in loads[4:]:
        copy.wait()
    pl.semaphore_wait(barrier, 3 + (n_yx - 1) + (n_dp - 1))
    for copy in halo:
        copy.start()

    put_kv(N, N)
    hid, sl = project(N, N, 2)
    put_heads(qcat, 0, hid)
    sl_q[...] = sl
    put_nrmt(N, N)
    loads[2].wait()
    loads[3].wait()
    ggs[...] = nt(cotv[...], wov[...])

    halo[0].wait_recv()
    halo[1].wait_recv()
    u_own = r["uv"][...].astype(F32)
    u_prev = jnp.where(s == 0, -1.0, uprev[...].astype(F32))
    g_own = r["gv"][...].astype(F32)
    g_prev = gprev[...].astype(F32)
    u_all = jnp.concatenate([u_prev, u_own], 1)
    g_all = jnp.broadcast_to(jnp.concatenate([g_prev, g_own], 1), (HD, 2 * N)).astype(BF)
    uc = jnp.transpose(jnp.broadcast_to(u_all, (HD, 2 * N)))[:, :1]
    freq = jnp.concatenate([r["fv"][...], r["fv"][...]], 1)
    mix = jnp.concatenate([r["mv"][...], r["mv"][...]], 1) * (HD**0.5)
    lane = lax.broadcasted_iota(jnp.int32, (1, HD), 1)
    shift = jnp.where(lane < HD // 2, 0.0, 0.5)

    def features(times):
        return cos_sin(times * freq, shift)

    for a in range(N // TQ):
        q0, k0 = a * TQ, a * TQ
        kpos = lax.broadcasted_iota(jnp.int32, (TQ, WIN), 1) + k0
        qpos = lax.broadcasted_iota(jnp.int32, (TQ, WIN), 0) + (q0 + N)
        same = uc[N + q0 : N + q0 + TQ, :] == u_all[:, k0 : k0 + WIN]
        mk = jnp.where(same & (kpos <= qpos), 1.0, 0.0)
        maskf[q0 : q0 + TQ, :] = 0.5 * mk
        feat = features(nt(mk.astype(BF), g_all[:, k0 : k0 + WIN]))
        cs_own[q0 : q0 + TQ, :] = feat
        fb = feat.astype(BF)
        for h in range(H):
            kcat[h, N + q0 : N + q0 + TQ, HD:] = fb
            qcat[h, q0 : q0 + TQ, HD:] = (feat * mix[h : h + 1, :]).astype(BF)
    pi = lax.broadcasted_iota(jnp.int32, (N, N), 0)
    pj = lax.broadcasted_iota(jnp.int32, (N, N), 1)
    mp = jnp.where((uc[:N, :] == u_all[:, :N]) & (pj <= pi), 1.0, 0.0).astype(BF)
    fb = features(nt(mp, g_all[:, :N])).astype(BF)
    for h in range(H):
        kcat[h, :N, HD:] = fb

    inv = HD**-0.5

    def piece(h, a, col, n):
        q0 = a * TQ
        k0 = q0 + col
        z = nt(qcat[h, q0 : q0 + TQ, :], kcat[h, k0 : k0 + n, :]) * inv
        sg = (jnp.tanh(0.5 * z) + 1.0) * maskf[q0 : q0 + TQ, col : col + n]
        wt = z * sg
        slp[h, q0 : q0 + TQ, col : col + n] = sg + wt * (1.0 - sg)
        wb = wt.astype(BF)
        wsav[h, q0 : q0 + TQ, col : col + n] = wb
        return nn(wb, v4[h, k0 : k0 + n, :])

    @pl.loop(0, H)
    def _(h):
        att4[h, :TQ, :] = piece(h, 0, N, TQ)
        att4[h, TQ:, :] = piece(h, 1, TQ, N)

    def halo_norm(at):
        wide, scale = norm(xp[at : at + TQ, :])
        nrm[at : at + TQ, :] = (wide * scale).astype(BF)
        put_kv(at, TQ)

    halo[2].wait_recv()
    halo_norm(TQ)

    @pl.loop(0, H)
    def _(h):
        att4[h, :TQ, :] += piece(h, 0, TQ, TQ)
        att4[h, TQ:, :] += piece(h, 1, 0, TQ)

    halo[3].wait_recv()
    halo_norm(0)

    @pl.loop(0, H)
    def _(h):
        att4[h, :TQ, :] += piece(h, 0, 0, TQ)

    attended = jnp.concatenate([att4[h] for h in range(H)], 1)
    scale_mid = lax.rsqrt(jnp.mean(attended * attended, -1, keepdims=True) + EPS)
    normed_mid = attended * scale_mid
    gate_wide = gate[...].astype(F32)
    gated = (normed_mid * gate_wide).astype(BF)
    gated_s[...] = gated
    t4 = jnp.transpose(gated).reshape(n_yx, 2, rows, N)
    for c in range(2):
        gatt[c] = t4[:, c].reshape(half, N)
    grad_gated = ggs[...]
    gpg[...] = (grad_gated * normed_mid * sl_g[...]).astype(BF)
    grad_mid = grad_gated * gate_wide
    ga = (
        scale_mid * (grad_mid - normed_mid * jnp.mean(grad_mid * normed_mid, -1, keepdims=True))
    ).astype(BF)
    for h in range(H):
        ga4[h] = ga[:, h * HD : (h + 1) * HD]

    w_h = 2 * HD
    tiles = (rows // 8) * (D // HD)
    per = tiles // n_dp

    def part(name, c):
        return r[c[0] + name].at[c[1]]

    def stage_copy(stage, c, src, dst, dev):
        i = c[1] + (0 if c[0] == "o" else 3)
        return remote(src, dst, r["st_ss"].at[stage, i], r["st_rs"].at[stage, i], dev)

    def whole(stage, c, ref):
        return stage_copy(stage, c, ref, ref, (dp, partner))

    waits = []

    def spread(stage, c, n, me, send):
        @pl.loop(1, n)
        def _(k):
            peer = lax.rem(me + k, n)
            src, dst, dev = send(peer)
            stage_copy(stage, c, src, dst, dev).start()

    def received(stage, c, ref, n):
        copy = whole(stage, c, ref.at[pl.ds(0, n - 1)])
        copy.wait_recv()
        waits.append(copy)

    def total_of(ref, n):
        total = ref[0].astype(F32)
        for i in range(1, n):
            total = total + ref[i].astype(F32)
        return total

    def s0_copy(c):
        return stage_copy(0, c, part("s0_s", c), part("s0_r", c), (dp, partner))

    def stage0(c, grad):
        shape = (n_yx, rows, D if c[0] == "o" else w_h)
        part("s0_s", c)[...] = grad(1 - core).reshape(shape).astype(BF)
        s0_copy(c).start()
        part("own", c)[...] = grad(core).reshape(shape)

    def pair_sum(c):
        copy = s0_copy(c)
        copy.wait_recv()
        waits.append(copy)
        return (part("own", c)[...] + part("s0_r", c)[...].astype(F32)).astype(BF)

    def h1(c):
        s_ref, r_ref = part("s1_s", c), part("s1_r", c)
        s_ref[...] = pair_sum(c)
        r_ref[m] = s_ref[m]
        spread(1, c, n_yx, m, lambda p: (s_ref.at[p], r_ref.at[m], yx_dev(p)))

    def o3(c):
        s_ref, r_ref = part("z_s", c), part("z_r", c)
        received(1, c, part("s1_r", c), n_yx)
        total = total_of(part("s1_r", c), n_yx).astype(BF)
        for i in range(tiles):
            at, col = i // (D // HD) * 8, i % (D // HD) * HD
            s_ref[i // per, i % per] = total[at : at + 8, col : col + HD]
        r_ref[dp] = s_ref[dp]
        spread(3, c, n_dp, dp, lambda p: (s_ref.at[p], r_ref.at[dp], z_dev(p)))

    def o4(c):
        r_ref = part("g_r", c)
        received(3, c, part("z_r", c), n_dp)
        r_ref[dp] = total_of(part("z_r", c), n_dp).astype(BF)
        spread(4, c, n_dp, dp, lambda p: (r_ref.at[dp], r_ref.at[dp], z_dev(p)))

    factor = float(n_dp * n_seq * N) ** -0.5

    def o5(c):
        r_ref = part("g_r", c)
        received(4, c, r_ref, n_dp)
        for i in range(tiles):
            at, col = i // (D // HD) * 8, i % (D // HD) * HD
            tile = r_ref[i // per, i % per].astype(F32) * factor
            if c[1] == 0:
                go_out[at : at + 8, col : col + HD] = tile
            else:
                base = (c[1] - 1) * D + col
                gp_out[at : at + 8, base : base + HD] = tile

    def h2(c):
        r_ref = part("z_r", c)
        received(1, c, part("s1_r", c), n_yx)
        r_ref[dp] = total_of(part("s1_r", c), n_yx).astype(BF)
        spread(2, c, n_dp, dp, lambda p: (r_ref.at[dp], r_ref.at[dp], z_dev(p)))

    def h3(c):
        received(2, c, part("z_r", c), n_dp)
        total = total_of(part("z_r", c), n_dp) * factor
        gp_out[:, 2 * D + c[1] * HD : 2 * D + (c[1] + 1) * HD] = total[:, :HD]
        gp_out[:, 3 * D + c[1] * HD : 3 * D + (c[1] + 1) * HD] = total[:, HD:]

    out_c, gate_c, val_c = ("o", 0), ("o", 1), ("o", 2)
    hc = [("h", h) for h in range(H)]
    stage0(out_c, lambda c: nn(gatt[c], cotv[...]))
    stage0(gate_c, lambda c: nn(nrmt[c, :, N:], gpg[...]))
    put_nrmt(0, N)

    def put_window(dst, t, sl, f, cols):
        dst[:TQ, cols] = (t[0][:TQ] * (sl[:TQ, cols] * f)).astype(BF)
        dst[TQ:WIN, cols] = ((t[0][TQ:] + t[1][:N]) * (sl[TQ:WIN, cols] * f)).astype(BF)
        dst[WIN:, cols] = (t[1][N:] * (sl[WIN:, cols] * f)).astype(BF)

    for h in range(H):
        t = [
            tn(wsav[h, q0 : q0 + TQ, :], ga4[h, q0 : q0 + TQ, :]) for q0 in range(0, N, TQ)
        ]
        put_window(gpv, t, sl_v, 1.0, slice(h * HD, (h + 1) * HD))
    h1(out_c)
    stage0(val_c, lambda c: nn(nrmt[c], gpv[...]))

    rowid = lax.broadcasted_iota(jnp.int32, (8, HD), 0)

    def head(h, tm, *between):
        cols = slice(h * HD, (h + 1) * HD)
        tk = []
        for a in range(N // TQ):
            q0, k0 = a * TQ, a * TQ
            gw = nt(ga4[h, q0 : q0 + TQ, :], v4[h, k0 : k0 + WIN, :])
            gs = (gw * slp[h, q0 : q0 + TQ, :]).astype(BF)
            tk.append(tn(gs, qcat[h, q0 : q0 + TQ, :HD]))
            dqc = nn(gs, kcat[h, k0 : k0 + WIN, :])
            gpq[q0 : q0 + TQ, cols] = (dqc[:, :HD] * (sl_q[q0 : q0 + TQ, cols] * inv)).astype(BF)
            got = jnp.sum(dqc[:, HD:] * cs_own[q0 : q0 + TQ, :], 0, keepdims=True)
            tm = tm + jnp.where(rowid == h, got, 0.0)
            if a == 0:
                for step, c in between:
                    step(c)
        put_window(gpk, tk, sl_k, inv, cols)
        return tm

    def head_grad(h):
        cols = slice(h * HD, (h + 1) * HD)

        def grad(c):
            own = nn(nrmt[c, :, N:], jnp.concatenate([gpq[:, cols], gpk[N:, cols]], 1))
            prev = nn(nrmt[c, :, :N], gpk[:N, cols])
            return jnp.concatenate([own[:, :HD], own[:, HD:] + prev], 1)

        return grad

    tm = head(0, jnp.zeros((8, HD), F32), (h1, gate_c))
    h1(val_c)
    stage0(hc[0], head_grad(0))
    tm = head(1, tm)
    h1(hc[0])
    stage0(hc[1], head_grad(1))
    tm = head(2, tm)
    h1(hc[1])
    stage0(hc[2], head_grad(2))
    tm = head(3, tm, (o3, out_c))
    h1(hc[2])
    t0_s[...] = tm
    tm0 = remote(t0_s, t0_r, tm_ss.at[0], tm_rs.at[0], (dp, partner))
    tm0.start()
    stage0(hc[3], head_grad(3))
    o3(gate_c)
    back_s[...] = (nt(gpv[:N, :], wv[:, D : 2 * D]) + nt(gpk[:N, :], wv[:, 3 * D :])).astype(BF)
    h1(hc[3])
    tm0.wait_recv()
    t1_r[m] = t0_s[...] + t0_r[...]

    @pl.loop(1, n_yx)
    def _(k):
        peer = lax.rem(m + k, n_yx)
        remote(t1_r.at[m], t1_r.at[m], tm_ss.at[1], tm_rs.at[1], yx_dev(peer)).start()

    back = remote(back_s, back_r, back_ss.at[0], back_rs.at[0], (dp, left))
    back.start()
    o3(val_c)
    h2(hc[0])
    lo_ref[...] = (xv[...].astype(F32) + nn(gated_s[...], wov[...])).astype(BF)
    ggs[...] = (
        nt(gpg[...], wv[:, :D])
        + nt(gpv[N:, :], wv[:, D : 2 * D])
        + nt(gpq[...], wv[:, 2 * D : 3 * D])
        + nt(gpk[N:, :], wv[:, 3 * D :])
    )
    h2(hc[1])
    o4(out_c)
    h2(hc[2])
    o4(gate_c)

    def tm_all(ref, i):
        return remote(ref, ref, tm_ss.at[i], tm_rs.at[i], (dp, partner))

    tm1, tm2 = tm_all(t1_r.at[pl.ds(0, n_yx - 1)], 1), tm_all(t2_r.at[pl.ds(0, n_dp - 1)], 2)
    tm1.wait_recv()
    tsum = t1_r[0]
    for i in range(1, n_yx):
        tsum = tsum + t1_r[i]
    t2_r[dp] = tsum

    @pl.loop(1, n_dp)
    def _(k):
        peer = lax.rem(dp + k, n_dp)
        remote(t2_r.at[dp], t2_r.at[dp], tm_ss.at[2], tm_rs.at[2], z_dev(peer)).start()

    o4(val_c)
    h2(hc[3])
    back.wait_recv()
    wide, scale = norm(xv[...])
    unit = wide * scale
    gn = ggs[...] + back_r[...].astype(F32)
    gi_ref[...] = (
        cotv[...].astype(F32) + scale * (gn - unit * jnp.mean(gn * unit, -1, keepdims=True))
    ).astype(BF)
    h3(hc[0])
    h3(hc[1])
    h3(hc[2])
    o5(out_c)
    o5(gate_c)
    o5(val_c)
    tm2.wait_recv()
    tsum = t2_r[0]
    for i in range(1, n_dp):
        tsum = tsum + t2_r[i]
    tsum = (tsum + pltpu.roll(tsum, HD // 2, 1)) * factor
    gt_out[...] = tsum[:H, : HD // 2]
    h3(hc[3])

    for copy in halo + [back, tm0, tm1, tm2] + waits:
        copy.wait_send()


def store(*refs):
    sems = refs[10]
    copies = [pltpu.make_async_copy(refs[i], refs[5 + i], sems.at[i]) for i in range(5)]
    for copy in copies:
        copy.start()
    for copy in copies:
        copy.wait()


def body(n_dp, n_seq, embeddings, user_ids, time_gaps, proj, out_w, freqs, mix, cot):
    n_yx = n_seq // 2
    rows = D // n_seq
    vm = pltpu.VMEM
    dma = pltpu.SemaphoreType.DMA
    scratch = {
        "xv": vm((N, D), BF),
        "xp": vm((N, D), BF),
        "wv": vm((D, 4 * D), BF),
        "wov": vm((D, D), BF),
        "cotv": vm((N, D), BF),
        "uprev": vm((1, N), jnp.int32),
        "gprev": vm((1, N), jnp.int32),
        "nrm": vm((2 * N, D), BF),
        "nrmt": vm((2, D // 2, 2 * N), BF),
        "gatt": vm((2, D // 2, N), BF),
        "sl_v": vm((2 * N, D), F32),
        "sl_k": vm((2 * N, D), F32),
        "sl_q": vm((N, D), F32),
        "sl_g": vm((N, D), F32),
        "gate": vm((N, D), BF),
        "kcat": vm((H, 2 * N, 2 * HD), BF),
        "qcat": vm((H, N, 2 * HD), BF),
        "v4": vm((H, 2 * N, HD), BF),
        "maskf": vm((N, WIN), F32),
        "cs_own": vm((N, HD), F32),
        "wsav": vm((H, N, WIN), BF),
        "slp": vm((H, N, WIN), F32),
        "att4": vm((H, N, HD), F32),
        "ggs": vm((N, D), F32),
        "ga4": vm((H, N, HD), BF),
        "gpv": vm((2 * N, D), BF),
        "gpk": vm((2 * N, D), BF),
        "gpq": vm((N, D), BF),
        "gpg": vm((N, D), BF),
        "gated_s": vm((N, D), BF),
        "back_s": vm((N, D), BF),
        "back_r": vm((N, D), BF),
        "t0_s": vm((8, HD), F32),
        "t0_r": vm((8, HD), F32),
        "t1_r": vm((n_yx, 8, HD), F32),
        "t2_r": vm((n_dp, 8, HD), F32),
        "uv": vm((1, N), jnp.int32),
        "gv": vm((1, N), jnp.int32),
        "fv": vm((1, HD // 2), F32),
        "mv": vm((H, HD // 2), F32),
        "in_sem": dma((8,)),
        "halo_ss": dma((4,)),
        "halo_rs": dma((4,)),
        "back_ss": dma((1,)),
        "back_rs": dma((1,)),
        "st_ss": dma((5, 3 + H)),
        "st_rs": dma((5, 3 + H)),
        "tm_ss": dma((3,)),
        "tm_rs": dma((3,)),
    }
    per = (rows // 8) * (D // HD) // n_dp
    for kind, count, width in (("o", 3, D), ("h", H, 2 * HD)):
        for name in ("s0_s", "s0_r", "s1_s", "s1_r"):
            scratch[kind + name] = vm((count, n_yx, rows, width), BF)
        scratch[kind + "own"] = vm((count, n_yx, rows, width), F32)
    for name in ("z_s", "z_r", "g_r"):
        scratch["o" + name] = vm((3, n_dp, per, 8, HD), BF)
    scratch["hz_r"] = vm((H, n_dp, rows, 2 * HD), BF)
    names = [str(i) for i in range(13)] + list(scratch)
    vspec = pl.BlockSpec(memory_space=pltpu.VMEM)
    hspec = pl.BlockSpec(memory_space=pltpu.HBM)
    results = (
        ((N, D), BF),
        ((N, D), BF),
        ((rows, 4 * D), F32),
        ((rows, D), F32),
        ((H, HD // 2), F32),
    )
    held = pl.pallas_call(
        functools.partial(kernel, n_dp, n_seq, names),
        out_shape=tuple(vm(shape, dtype) for shape, dtype in results),
        in_specs=[hspec] * 8,
        out_specs=(vspec,) * 5,
        scratch_shapes=list(scratch.values()),
        compiler_params=pltpu.CompilerParams(
            collective_id=0, has_side_effects=True, vmem_limit_bytes=56 * 1024 * 1024
        ),
        name="layer",
    )(embeddings[0], user_ids, time_gaps, proj, out_w, freqs[None], mix, cot[0])
    lo, gi, gp, go, gt = pl.pallas_call(
        store,
        out_shape=tuple(jax.ShapeDtypeStruct(shape, dtype) for shape, dtype in results),
        in_specs=[vspec] * 5,
        out_specs=(hspec,) * 5,
        scratch_shapes=[dma((5,))],
        compiler_params=pltpu.CompilerParams(vmem_limit_bytes=4 * 1024 * 1024),
        name="store",
    )(*held)
    return lo[None], gi[None], gp, go, gt


def solution(mesh):
    n_dp, n_seq = mesh.shape["dp"], mesh.shape["seq"]
    return jax.shard_map(
        functools.partial(body, n_dp, n_seq),
        mesh=mesh,
        in_specs=(
            P("dp", "seq", None),
            P("dp", "seq"),
            P("dp", "seq"),
            P(),
            P(),
            P(),
            P(),
            P("dp", "seq", None),
        ),
        out_specs=(P("dp", "seq", None), P("dp", "seq", None), P("seq", None), P("seq", None), P()),
        check_vma=False,
    )
```

```python
import functools

import jax
import jax.numpy as jnp
from jax import lax
from jax.experimental import pallas as pl
from jax.experimental.pallas import tpu as pltpu
from jax.sharding import PartitionSpec as P

EPS = 1e-05
F32 = jnp.float32
BF = jnp.bfloat16
N = 512
D = 512
H = 4
HD = 128
TQ = 256
WIN = 768
MESH = pl.DeviceIdType.MESH


def nn(a, b):
    return lax.dot_general(a, b, (((1,), (0,)), ((), ())), preferred_element_type=F32)


def nt(a, b):
    return lax.dot_general(a, b, (((1,), (1,)), ((), ())), preferred_element_type=F32)


def tn(a, b):
    return lax.dot_general(a, b, (((0,), (0,)), ((), ())), preferred_element_type=F32)


def sigmoid(z):
    return 0.5 * jnp.tanh(0.5 * z) + 0.5


COS = (1.0, -1 / 2, 1 / 24, -1 / 720, 1 / 40320, -1 / 3628800, 1 / 479001600)
PI_PARTS = (3.140625, 9.67502593994140625e-4, 1.509957990978376432e-7)


def cos_sin(ang, half):
    k = jnp.floor(ang * (1.0 / 3.141592653589793) - half + 0.5)
    c = k + half
    r = ((ang - c * PI_PARTS[0]) - c * PI_PARTS[1]) - c * PI_PARTS[2]
    r2 = r * r
    p = jnp.full_like(r2, COS[-1])
    for q in COS[-2::-1]:
        p = p * r2 + q
    odd = k * 0.5
    odd = odd - jnp.floor(odd)
    return p * (1.0 - 4.0 * odd)


def kernel(n_dp, n_seq, names, *refs):
    r = dict(zip(names, refs))
    x_ref, u_ref, g_ref, w_ref, wo_ref, f_ref, mix_ref, cot_ref = refs[:8]
    lo_ref, gi_ref, gp_out, go_out, gt_out = refs[8:13]
    xv, xp, wv, wov, cotv = r["xv"], r["xp"], r["wv"], r["wov"], r["cotv"]
    uprev, gprev = r["uprev"], r["gprev"]
    nrm, nrmt, gatt = r["nrm"], r["nrmt"], r["gatt"]
    sl_v, sl_k, sl_q, sl_g = r["sl_v"], r["sl_k"], r["sl_q"], r["sl_g"]
    gate, kcat, qcat, v4 = r["gate"], r["kcat"], r["qcat"], r["v4"]
    maskf, cs_own, wsav, slp, att4 = r["maskf"], r["cs_own"], r["wsav"], r["slp"], r["att4"]
    ggs, ga4, gpv, gpk, gpq, gpg = r["ggs"], r["ga4"], r["gpv"], r["gpk"], r["gpq"], r["gpg"]
    back_s, back_r, gated_s = r["back_s"], r["back_r"], r["gated_s"]
    t0_s, t0_r, t1_r, t2_r = r["t0_s"], r["t0_r"], r["t1_r"], r["t2_r"]
    in_sem, halo_ss, halo_rs = r["in_sem"], r["halo_ss"], r["halo_rs"]
    back_ss, back_rs, tm_ss, tm_rs = r["back_ss"], r["back_rs"], r["tm_ss"], r["tm_rs"]

    n_yx = n_seq // 2
    rows = D // n_seq
    half = D // 2
    dp = lax.axis_index("dp")
    s = lax.axis_index("seq")
    core = lax.rem(s, 2)
    m = lax.div(s, 2)
    right = lax.rem(s + 1, n_seq)
    left = lax.rem(s + n_seq - 1, n_seq)
    partner = m * 2 + 1 - core

    def yx_dev(i):
        return (dp, i * 2 + core)

    def z_dev(i):
        return (i, s)

    barrier = pltpu.get_barrier_semaphore()
    for peer in (left, right, partner):
        pl.semaphore_signal(barrier, inc=1, device_id=(dp, peer), device_id_type=MESH)

    @pl.loop(1, n_yx)
    def _(k):
        peer = lax.rem(m + k, n_yx)
        pl.semaphore_signal(barrier, inc=1, device_id=yx_dev(peer), device_id_type=MESH)

    @pl.loop(1, n_dp)
    def _(k):
        peer = lax.rem(dp + k, n_dp)
        pl.semaphore_signal(barrier, inc=1, device_id=z_dev(peer), device_id_type=MESH)

    loads = [
        pltpu.make_async_copy(x_ref, xv, in_sem.at[0]),
        pltpu.make_async_copy(w_ref, wv, in_sem.at[1]),
        pltpu.make_async_copy(wo_ref, wov, in_sem.at[2]),
        pltpu.make_async_copy(cot_ref, cotv, in_sem.at[3]),
        pltpu.make_async_copy(u_ref, r["uv"], in_sem.at[4]),
        pltpu.make_async_copy(g_ref, r["gv"], in_sem.at[5]),
        pltpu.make_async_copy(f_ref, r["fv"], in_sem.at[6]),
        pltpu.make_async_copy(mix_ref, r["mv"], in_sem.at[7]),
    ]
    for copy in loads:
        copy.start()

    def remote(src, dst, ss, rs, dev):
        return pltpu.make_async_remote_copy(
            src_ref=src, dst_ref=dst, send_sem=ss, recv_sem=rs, device_id=dev, device_id_type=MESH
        )

    hi, lo = pl.ds(TQ, TQ), pl.ds(0, TQ)
    halo = [
        remote(r["uv"], uprev, halo_ss.at[0], halo_rs.at[0], (dp, right)),
        remote(r["gv"], gprev, halo_ss.at[1], halo_rs.at[1], (dp, right)),
        remote(xv.at[hi], xp.at[hi], halo_ss.at[2], halo_rs.at[2], (dp, right)),
        remote(xv.at[lo], xp.at[lo], halo_ss.at[3], halo_rs.at[3], (dp, right)),
    ]

    def norm(x):
        wide = x.astype(F32)
        scale = lax.rsqrt(jnp.mean(wide * wide, -1, keepdims=True) + EPS)
        return wide, scale

    def project(at, n, group):
        p = nn(nrm[at : at + n, :], wv[:, group * D : (group + 1) * D])
        sg = sigmoid(p)
        hid = p * sg
        return hid.astype(BF), sg + hid * (1.0 - sg)

    def put_heads(dst, at, val):
        n = val.shape[0]
        for h in range(H):
            dst[h, at : at + n, :HD] = val[:, h * HD : (h + 1) * HD]

    def put_kv(at, n):
        hid, sl = project(at, n, 1)
        put_heads(v4, at, hid)
        sl_v[at : at + n, :] = sl
        hid, sl = project(at, n, 3)
        put_heads(kcat, at, hid)
        sl_k[at : at + n, :] = sl

    def put_nrmt(at, n):
        t4 = jnp.transpose(nrm[at : at + n, :]).reshape(n_yx, 2, rows, n)
        for c in range(2):
            nrmt[c, :, at : at + n] = t4[:, c].reshape(half, n)

    loads[0].wait()
    wide, scale = norm(xv[...])
    nrm[N:, :] = (wide * scale).astype(BF)
    loads[1].wait()
    hid, sl = project(N, N, 0)
    gate[...] = hid
    sl_g[...] = sl

    for copy in loads[4:]:
        copy.wait()
    pl.semaphore_wait(barrier, 3 + (n_yx - 1) + (n_dp - 1))
    for copy in halo:
        copy.start()

    put_kv(N, N)
    hid, sl = project(N, N, 2)
    put_heads(qcat, 0, hid)
    sl_q[...] = sl
    put_nrmt(N, N)
    loads[2].wait()
    loads[3].wait()
    ggs[...] = nt(cotv[...], wov[...])

    halo[0].wait_recv()
    halo[1].wait_recv()
    u_own = r["uv"][...].astype(F32)
    u_prev = jnp.where(s == 0, -1.0, uprev[...].astype(F32))
    g_own = r["gv"][...].astype(F32)
    g_prev = gprev[...].astype(F32)
    u_all = jnp.concatenate([u_prev, u_own], 1)
    g_all = jnp.broadcast_to(jnp.concatenate([g_prev, g_own], 1), (HD, 2 * N)).astype(BF)
    uc = jnp.transpose(jnp.broadcast_to(u_all, (HD, 2 * N)))[:, :1]
    freq = jnp.concatenate([r["fv"][...], r["fv"][...]], 1)
    mix = jnp.concatenate([r["mv"][...], r["mv"][...]], 1) * (HD**0.5)
    lane = lax.broadcasted_iota(jnp.int32, (1, HD), 1)
    shift = jnp.where(lane < HD // 2, 0.0, 0.5)

    def features(times):
        return cos_sin(times * freq, shift)

    for a in range(N // TQ):
        q0, k0 = a * TQ, a * TQ
        kpos = lax.broadcasted_iota(jnp.int32, (TQ, WIN), 1) + k0
        qpos = lax.broadcasted_iota(jnp.int32, (TQ, WIN), 0) + (q0 + N)
        same = uc[N + q0 : N + q0 + TQ, :] == u_all[:, k0 : k0 + WIN]
        mk = jnp.where(same & (kpos <= qpos), 1.0, 0.0)
        maskf[q0 : q0 + TQ, :] = 0.5 * mk
        feat = features(nt(mk.astype(BF), g_all[:, k0 : k0 + WIN]))
        cs_own[q0 : q0 + TQ, :] = feat
        fb = feat.astype(BF)
        for h in range(H):
            kcat[h, N + q0 : N + q0 + TQ, HD:] = fb
            qcat[h, q0 : q0 + TQ, HD:] = (feat * mix[h : h + 1, :]).astype(BF)
    pi = lax.broadcasted_iota(jnp.int32, (N, N), 0)
    pj = lax.broadcasted_iota(jnp.int32, (N, N), 1)
    mp = jnp.where((uc[:N, :] == u_all[:, :N]) & (pj <= pi), 1.0, 0.0).astype(BF)
    fb = features(nt(mp, g_all[:, :N])).astype(BF)
    for h in range(H):
        kcat[h, :N, HD:] = fb

    inv = HD**-0.5

    def piece(h, a, col, n):
        q0 = a * TQ
        k0 = q0 + col
        z = nt(qcat[h, q0 : q0 + TQ, :], kcat[h, k0 : k0 + n, :]) * inv
        sg = (jnp.tanh(0.5 * z) + 1.0) * maskf[q0 : q0 + TQ, col : col + n]
        wt = z * sg
        slp[h, q0 : q0 + TQ, col : col + n] = sg + wt * (1.0 - sg)
        wb = wt.astype(BF)
        wsav[h, q0 : q0 + TQ, col : col + n] = wb
        return nn(wb, v4[h, k0 : k0 + n, :])

    @pl.loop(0, H)
    def _(h):
        att4[h, :TQ, :] = piece(h, 0, N, TQ)
        att4[h, TQ:, :] = piece(h, 1, TQ, N)

    def halo_norm(at):
        wide, scale = norm(xp[at : at + TQ, :])
        nrm[at : at + TQ, :] = (wide * scale).astype(BF)
        put_kv(at, TQ)

    halo[2].wait_recv()
    halo_norm(TQ)

    @pl.loop(0, H)
    def _(h):
        att4[h, :TQ, :] += piece(h, 0, TQ, TQ)
        att4[h, TQ:, :] += piece(h, 1, 0, TQ)

    halo[3].wait_recv()
    halo_norm(0)

    @pl.loop(0, H)
    def _(h):
        att4[h, :TQ, :] += piece(h, 0, 0, TQ)

    attended = jnp.concatenate([att4[h] for h in range(H)], 1)
    scale_mid = lax.rsqrt(jnp.mean(attended * attended, -1, keepdims=True) + EPS)
    normed_mid = attended * scale_mid
    gate_wide = gate[...].astype(F32)
    gated = (normed_mid * gate_wide).astype(BF)
    gated_s[...] = gated
    t4 = jnp.transpose(gated).reshape(n_yx, 2, rows, N)
    for c in range(2):
        gatt[c] = t4[:, c].reshape(half, N)
    grad_gated = ggs[...]
    gpg[...] = (grad_gated * normed_mid * sl_g[...]).astype(BF)
    grad_mid = grad_gated * gate_wide
    ga = (
        scale_mid * (grad_mid - normed_mid * jnp.mean(grad_mid * normed_mid, -1, keepdims=True))
    ).astype(BF)
    for h in range(H):
        ga4[h] = ga[:, h * HD : (h + 1) * HD]

    w_h = 2 * HD
    tiles = (rows // 8) * (D // HD)
    per = tiles // n_dp

    def part(name, c):
        return r[c[0] + name].at[c[1]]

    def stage_copy(stage, c, src, dst, dev):
        i = c[1] + (0 if c[0] == "o" else 3)
        return remote(src, dst, r["st_ss"].at[stage, i], r["st_rs"].at[stage, i], dev)

    def whole(stage, c, ref):
        return stage_copy(stage, c, ref, ref, (dp, partner))

    waits = []

    def spread(stage, c, n, me, send):
        @pl.loop(0, n - 1)
        def _(k):
            peer = lax.rem(me + 1 + lax.rem(k + n // 2 - 1, n - 1), n)
            src, dst, dev = send(peer)
            stage_copy(stage, c, src, dst, dev).start()

    def received(stage, c, ref, n):
        copy = whole(stage, c, ref.at[pl.ds(0, n - 1)])
        copy.wait_recv()
        waits.append(copy)

    def total_of(ref, n):
        total = ref[0].astype(F32)
        for i in range(1, n):
            total = total + ref[i].astype(F32)
        return total

    def s0_copy(c):
        return stage_copy(0, c, part("s0_s", c), part("s0_r", c), (dp, partner))

    def stage0(c, grad):
        shape = (n_yx, rows, D if c[0] == "o" else w_h)
        part("s0_s", c)[...] = grad(1 - core).reshape(shape).astype(BF)
        s0_copy(c).start()
        part("own", c)[...] = grad(core).reshape(shape)

    def pair_sum(c):
        copy = s0_copy(c)
        copy.wait_recv()
        waits.append(copy)
        return (part("own", c)[...] + part("s0_r", c)[...].astype(F32)).astype(BF)

    def h1(c):
        s_ref, r_ref = part("s1_s", c), part("s1_r", c)
        s_ref[...] = pair_sum(c)
        r_ref[m] = s_ref[m]
        spread(1, c, n_yx, m, lambda p: (s_ref.at[p], r_ref.at[m], yx_dev(p)))

    def o3(c):
        s_ref, r_ref = part("z_s", c), part("z_r", c)
        received(1, c, part("s1_r", c), n_yx)
        total = total_of(part("s1_r", c), n_yx).astype(BF)
        for i in range(tiles):
            at, col = i // (D // HD) * 8, i % (D // HD) * HD
            s_ref[i // per, i % per] = total[at : at + 8, col : col + HD]
        r_ref[dp] = s_ref[dp]
        spread(3, c, n_dp, dp, lambda p: (s_ref.at[p], r_ref.at[dp], z_dev(p)))

    def o4(c):
        r_ref = part("g_r", c)
        received(3, c, part("z_r", c), n_dp)
        r_ref[dp] = total_of(part("z_r", c), n_dp).astype(BF)
        spread(4, c, n_dp, dp, lambda p: (r_ref.at[dp], r_ref.at[dp], z_dev(p)))

    factor = float(n_dp * n_seq * N) ** -0.5

    def o5(c):
        r_ref = part("g_r", c)
        received(4, c, r_ref, n_dp)
        for i in range(tiles):
            at, col = i // (D // HD) * 8, i % (D // HD) * HD
            tile = r_ref[i // per, i % per].astype(F32) * factor
            if c[1] == 0:
                go_out[at : at + 8, col : col + HD] = tile
            else:
                base = (c[1] - 1) * D + col
                gp_out[at : at + 8, base : base + HD] = tile

    def h2(c):
        r_ref = part("z_r", c)
        received(1, c, part("s1_r", c), n_yx)
        r_ref[dp] = total_of(part("s1_r", c), n_yx).astype(BF)
        spread(2, c, n_dp, dp, lambda p: (r_ref.at[dp], r_ref.at[dp], z_dev(p)))

    def h3(c):
        received(2, c, part("z_r", c), n_dp)
        total = total_of(part("z_r", c), n_dp) * factor
        gp_out[:, 2 * D + c[1] * HD : 2 * D + (c[1] + 1) * HD] = total[:, :HD]
        gp_out[:, 3 * D + c[1] * HD : 3 * D + (c[1] + 1) * HD] = total[:, HD:]

    out_c, gate_c, val_c = ("o", 0), ("o", 1), ("o", 2)
    hc = [("h", h) for h in range(H)]
    stage0(out_c, lambda c: nn(gatt[c], cotv[...]))
    stage0(gate_c, lambda c: nn(nrmt[c, :, N:], gpg[...]))
    put_nrmt(0, N)

    def put_window(dst, t, sl, f, cols):
        dst[:TQ, cols] = (t[0][:TQ] * (sl[:TQ, cols] * f)).astype(BF)
        dst[TQ:WIN, cols] = ((t[0][TQ:] + t[1][:N]) * (sl[TQ:WIN, cols] * f)).astype(BF)
        dst[WIN:, cols] = (t[1][N:] * (sl[WIN:, cols] * f)).astype(BF)

    for h in range(H):
        t = [
            tn(wsav[h, q0 : q0 + TQ, :], ga4[h, q0 : q0 + TQ, :]) for q0 in range(0, N, TQ)
        ]
        put_window(gpv, t, sl_v, 1.0, slice(h * HD, (h + 1) * HD))
    h1(out_c)
    stage0(val_c, lambda c: nn(nrmt[c], gpv[...]))

    rowid = lax.broadcasted_iota(jnp.int32, (8, HD), 0)

    def head(h, tm, *between):
        cols = slice(h * HD, (h + 1) * HD)
        tk = []
        for a in range(N // TQ):
            q0, k0 = a * TQ, a * TQ
            gw = nt(ga4[h, q0 : q0 + TQ, :], v4[h, k0 : k0 + WIN, :])
            gs = (gw * slp[h, q0 : q0 + TQ, :]).astype(BF)
            tk.append(tn(gs, qcat[h, q0 : q0 + TQ, :HD]))
            dqc = nn(gs, kcat[h, k0 : k0 + WIN, :])
            gpq[q0 : q0 + TQ, cols] = (dqc[:, :HD] * (sl_q[q0 : q0 + TQ, cols] * inv)).astype(BF)
            got = jnp.sum(dqc[:, HD:] * cs_own[q0 : q0 + TQ, :], 0, keepdims=True)
            tm = tm + jnp.where(rowid == h, got, 0.0)
            if a == 0:
                for step, c in between:
                    step(c)
        put_window(gpk, tk, sl_k, inv, cols)
        return tm

    def head_grad(h):
        cols = slice(h * HD, (h + 1) * HD)

        def grad(c):
            own = nn(nrmt[c, :, N:], jnp.concatenate([gpq[:, cols], gpk[N:, cols]], 1))
            prev = nn(nrmt[c, :, :N], gpk[:N, cols])
            return jnp.concatenate([own[:, :HD], own[:, HD:] + prev], 1)

        return grad

    tm = head(0, jnp.zeros((8, HD), F32), (h1, gate_c))
    h1(val_c)
    stage0(hc[0], head_grad(0))
    tm = head(1, tm)
    h1(hc[0])
    stage0(hc[1], head_grad(1))
    tm = head(2, tm)
    h1(hc[1])
    stage0(hc[2], head_grad(2))
    tm = head(3, tm, (o3, out_c))
    h1(hc[2])
    t0_s[...] = tm
    tm0 = remote(t0_s, t0_r, tm_ss.at[0], tm_rs.at[0], (dp, partner))
    tm0.start()
    stage0(hc[3], head_grad(3))
    o3(gate_c)
    back_s[...] = (nt(gpv[:N, :], wv[:, D : 2 * D]) + nt(gpk[:N, :], wv[:, 3 * D :])).astype(BF)
    h1(hc[3])
    tm0.wait_recv()
    t1_r[m] = t0_s[...] + t0_r[...]

    @pl.loop(1, n_yx)
    def _(k):
        peer = lax.rem(m + k, n_yx)
        remote(t1_r.at[m], t1_r.at[m], tm_ss.at[1], tm_rs.at[1], yx_dev(peer)).start()

    back = remote(back_s, back_r, back_ss.at[0], back_rs.at[0], (dp, left))
    back.start()
    o3(val_c)
    h2(hc[0])
    lo_ref[...] = (xv[...].astype(F32) + nn(gated_s[...], wov[...])).astype(BF)
    ggs[...] = (
        nt(gpg[...], wv[:, :D])
        + nt(gpv[N:, :], wv[:, D : 2 * D])
        + nt(gpq[...], wv[:, 2 * D : 3 * D])
        + nt(gpk[N:, :], wv[:, 3 * D :])
    )
    h2(hc[1])
    o4(out_c)
    h2(hc[2])
    o4(gate_c)

    def tm_all(ref, i):
        return remote(ref, ref, tm_ss.at[i], tm_rs.at[i], (dp, partner))

    tm1, tm2 = tm_all(t1_r.at[pl.ds(0, n_yx - 1)], 1), tm_all(t2_r.at[pl.ds(0, n_dp - 1)], 2)
    tm1.wait_recv()
    tsum = t1_r[0]
    for i in range(1, n_yx):
        tsum = tsum + t1_r[i]
    t2_r[dp] = tsum

    @pl.loop(1, n_dp)
    def _(k):
        peer = lax.rem(dp + k, n_dp)
        remote(t2_r.at[dp], t2_r.at[dp], tm_ss.at[2], tm_rs.at[2], z_dev(peer)).start()

    o4(val_c)
    h2(hc[3])
    back.wait_recv()
    wide, scale = norm(xv[...])
    unit = wide * scale
    gn = ggs[...] + back_r[...].astype(F32)
    gi_ref[...] = (
        cotv[...].astype(F32) + scale * (gn - unit * jnp.mean(gn * unit, -1, keepdims=True))
    ).astype(BF)
    h3(hc[0])
    h3(hc[1])
    h3(hc[2])
    o5(out_c)
    o5(gate_c)
    o5(val_c)
    tm2.wait_recv()
    tsum = t2_r[0]
    for i in range(1, n_dp):
        tsum = tsum + t2_r[i]
    tsum = (tsum + pltpu.roll(tsum, HD // 2, 1)) * factor
    gt_out[...] = tsum[:H, : HD // 2]
    h3(hc[3])

    for copy in halo + [back, tm0, tm1, tm2] + waits:
        copy.wait_send()


def store(*refs):
    sems = refs[10]
    copies = [pltpu.make_async_copy(refs[i], refs[5 + i], sems.at[i]) for i in range(5)]
    for copy in copies:
        copy.start()
    for copy in copies:
        copy.wait()


def body(n_dp, n_seq, embeddings, user_ids, time_gaps, proj, out_w, freqs, mix, cot):
    n_yx = n_seq // 2
    rows = D // n_seq
    vm = pltpu.VMEM
    dma = pltpu.SemaphoreType.DMA
    scratch = {
        "xv": vm((N, D), BF),
        "xp": vm((N, D), BF),
        "wv": vm((D, 4 * D), BF),
        "wov": vm((D, D), BF),
        "cotv": vm((N, D), BF),
        "uprev": vm((1, N), jnp.int32),
        "gprev": vm((1, N), jnp.int32),
        "nrm": vm((2 * N, D), BF),
        "nrmt": vm((2, D // 2, 2 * N), BF),
        "gatt": vm((2, D // 2, N), BF),
        "sl_v": vm((2 * N, D), F32),
        "sl_k": vm((2 * N, D), F32),
        "sl_q": vm((N, D), F32),
        "sl_g": vm((N, D), F32),
        "gate": vm((N, D), BF),
        "kcat": vm((H, 2 * N, 2 * HD), BF),
        "qcat": vm((H, N, 2 * HD), BF),
        "v4": vm((H, 2 * N, HD), BF),
        "maskf": vm((N, WIN), F32),
        "cs_own": vm((N, HD), F32),
        "wsav": vm((H, N, WIN), BF),
        "slp": vm((H, N, WIN), F32),
        "att4": vm((H, N, HD), F32),
        "ggs": vm((N, D), F32),
        "ga4": vm((H, N, HD), BF),
        "gpv": vm((2 * N, D), BF),
        "gpk": vm((2 * N, D), BF),
        "gpq": vm((N, D), BF),
        "gpg": vm((N, D), BF),
        "gated_s": vm((N, D), BF),
        "back_s": vm((N, D), BF),
        "back_r": vm((N, D), BF),
        "t0_s": vm((8, HD), F32),
        "t0_r": vm((8, HD), F32),
        "t1_r": vm((n_yx, 8, HD), F32),
        "t2_r": vm((n_dp, 8, HD), F32),
        "uv": vm((1, N), jnp.int32),
        "gv": vm((1, N), jnp.int32),
        "fv": vm((1, HD // 2), F32),
        "mv": vm((H, HD // 2), F32),
        "in_sem": dma((8,)),
        "halo_ss": dma((4,)),
        "halo_rs": dma((4,)),
        "back_ss": dma((1,)),
        "back_rs": dma((1,)),
        "st_ss": dma((5, 3 + H)),
        "st_rs": dma((5, 3 + H)),
        "tm_ss": dma((3,)),
        "tm_rs": dma((3,)),
    }
    per = (rows // 8) * (D // HD) // n_dp
    for kind, count, width in (("o", 3, D), ("h", H, 2 * HD)):
        for name in ("s0_s", "s0_r", "s1_s", "s1_r"):
            scratch[kind + name] = vm((count, n_yx, rows, width), BF)
        scratch[kind + "own"] = vm((count, n_yx, rows, width), F32)
    for name in ("z_s", "z_r", "g_r"):
        scratch["o" + name] = vm((3, n_dp, per, 8, HD), BF)
    scratch["hz_r"] = vm((H, n_dp, rows, 2 * HD), BF)
    names = [str(i) for i in range(13)] + list(scratch)
    vspec = pl.BlockSpec(memory_space=pltpu.VMEM)
    hspec = pl.BlockSpec(memory_space=pltpu.HBM)
    results = (
        ((N, D), BF),
        ((N, D), BF),
        ((rows, 4 * D), F32),
        ((rows, D), F32),
        ((H, HD // 2), F32),
    )
    held = pl.pallas_call(
        functools.partial(kernel, n_dp, n_seq, names),
        out_shape=tuple(vm(shape, dtype) for shape, dtype in results),
        in_specs=[hspec] * 8,
        out_specs=(vspec,) * 5,
        scratch_shapes=list(scratch.values()),
        compiler_params=pltpu.CompilerParams(
            collective_id=0, has_side_effects=True, vmem_limit_bytes=56 * 1024 * 1024
        ),
        name="layer",
    )(embeddings[0], user_ids, time_gaps, proj, out_w, freqs[None], mix, cot[0])
    lo, gi, gp, go, gt = pl.pallas_call(
        store,
        out_shape=tuple(jax.ShapeDtypeStruct(shape, dtype) for shape, dtype in results),
        in_specs=[vspec] * 5,
        out_specs=(hspec,) * 5,
        scratch_shapes=[dma((5,))],
        compiler_params=pltpu.CompilerParams(vmem_limit_bytes=4 * 1024 * 1024),
        name="store",
    )(*held)
    return lo[None], gi[None], gp, go, gt


def solution(mesh):
    n_dp, n_seq = mesh.shape["dp"], mesh.shape["seq"]
    return jax.shard_map(
        functools.partial(body, n_dp, n_seq),
        mesh=mesh,
        in_specs=(
            P("dp", "seq", None),
            P("dp", "seq"),
            P("dp", "seq"),
            P(),
            P(),
            P(),
            P(),
            P("dp", "seq", None),
        ),
        out_specs=(P("dp", "seq", None), P("dp", "seq", None), P("seq", None), P("seq", None), P()),
        check_vma=False,
    )
```
